512 devices in a mesh: pool: 128 (over z, y, core), mlp: 4 (over x).
Axes of the slice: x: 4, y: 8, z: 8, core: 2. Of those that a mesh axis runs over, the one named last changes fastest.
Arguments:
- residual_in: bfloat16 [256, 3072], P('pool', 'mlp'), may hold values from -6 to 6
- query_new: bfloat16 [256, 3072], P('pool', 'mlp'), may hold values from -6 to 6
- key_new: bfloat16 [256, 3072], P('pool', 'mlp'), may hold values from -6 to 6
- value_new: bfloat16 [256, 3072], P('pool', 'mlp'), may hold values from -6 to 6
- key_cache: bfloat16 [640, 256, 3072], P('pool', None, 'mlp'), may hold values from -240 to 240
- value_cache: bfloat16 [640, 256, 3072], P('pool', None, 'mlp'), may hold values from -6 to 6
- block_table: int32 [256, 8], P('pool'), may hold values from -1 to 639, as said below
- lengths: int32 [256], P('pool'), may hold values from 1 to 2048, as said below
- out_weight: bfloat16 [3072, 3072], P('mlp', 'pool'), may hold values from -0.109375 to 0.109375
- norm_gain: bfloat16 [3072], P('mlp'), may hold values from 0.25 to 1.75
- gate_weight: bfloat16 [3072, 8192], P('mlp', 'pool'), may hold values from -0.109375 to 0.109375
- up_weight: bfloat16 [3072, 8192], P('mlp', 'pool'), may hold values from -0.109375 to 0.109375
- down_weight: bfloat16 [8192, 3072], P('pool', 'mlp'), may hold values from -0.0625 to 0.0625
Outputs:
- layer_out: bfloat16 [256, 3072], P('pool', 'mlp')
The draws below stay inside these ranges and needn't reach their ends.
Inputs may be any that keep to these rules, and one draw needn't show every extreme that they name: `block_table`: row r lists ceil(lengths[r] / 256) distinct block numbers followed by -1; no block is listed twice in the whole table. `lengths`: some request holds exactly 2048 tokens.
All inputs are finite; a program needn't handle non-finite values.
Results may differ from the reference program's by a relative error of at most 0.012.
Values may be sent and summed in bfloat16 or wider, within the bound.
A program may use at most 64 MiB of HBM per device.

```python
import math
import jax
import jax.numpy as jnp
from jax import lax

H = 32
HD = 96
D = 3072
FF = 8192
BT = 256
MAXB = 8
REQ = 256
BLOCKS = 640


def block_layout(key):
    layout_key = jax.random.fold_in(key, 7)
    key_count, key_heavy, key_tail, key_order = jax.random.split(layout_key, 4)
    request_ids = jnp.arange(REQ, dtype=jnp.int32)
    counts = jax.random.randint(key_count, (REQ,), 1, 3).astype(jnp.int32)
    heavy_row = jax.random.randint(key_heavy, (), 0, REQ).astype(jnp.int32)
    counts = jnp.where(request_ids == heavy_row, MAXB, counts)
    tail_len = jax.random.randint(key_tail, (REQ,), 1, BT + 1).astype(jnp.int32)
    tail_len = jnp.where(request_ids == heavy_row, BT, tail_len)
    lengths = (counts - 1) * BT + tail_len
    shuffled = jax.random.permutation(key_order, jnp.arange(BLOCKS, dtype=jnp.int32))
    first_slot = jnp.cumsum(counts) - counts
    slot_ids = first_slot[:, None] + jnp.arange(MAXB, dtype=jnp.int32)[None, :]
    block_ids = shuffled[jnp.clip(slot_ids, 0, BLOCKS - 1)]
    block_ids = jnp.where(jnp.arange(MAXB, dtype=jnp.int32)[None, :] < counts[:, None], block_ids, -1)
    return (block_ids.astype(jnp.int32), lengths.astype(jnp.int32))


def draw_block_table(key, part):
    return block_layout(key)[0]


def draw_lengths(key, part):
    return block_layout(key)[1]


def draw_key_cache(key, part):
    entries = jnp.clip(jax.random.normal(key, (BLOCKS, BT, D), jnp.float32), -6.0, 6.0)
    return entries.astype(jnp.bfloat16)


def block_levels(rng, shape, cuts, least, high):
    factor_of = 1.0
    for axis_at, shards_of in cuts:
        draws = jax.random.uniform(jax.random.fold_in(jax.random.fold_in(rng, 6), axis_at), (shards_of,), jnp.float32, least / len(cuts), high / len(cuts))
        factor_of = factor_of * jnp.repeat(jnp.exp(draws), shape[axis_at] // shards_of).reshape((-1,) + (1,) * (len(shape) - 1 - axis_at))
    return factor_of


def noise(key, extent, spread, most, cuts=(), kind=jnp.bfloat16):
    level = block_levels(key, extent, cuts, -0.22, 0.18) if cuts else 1.0
    values = jax.random.normal(key, extent, jnp.float32) * spread * level
    return jnp.minimum(jnp.maximum(values, -most), most).astype(kind)


def setup_inputs(seed: int = 0) -> dict:
    key_list = jax.random.split(jax.random.key(seed), 14)
    return {
        "residual_in": noise(key_list[0], (REQ, D), 1.0, 6.0, ((0, 128), (1, 4))),
        "query_new": noise(key_list[1], (REQ, D), 1.0, 6.0, ((0, 128), (1, 4))),
        "key_new": noise(key_list[2], (REQ, D), 1.0, 6.0, ((0, 128), (1, 4))),
        "value_new": noise(key_list[3], (REQ, D), 1.0, 6.0, ((0, 128), (1, 4))),
        "key_cache": draw_key_cache(jax.random.fold_in(key_list[13], 71), 0),
        "value_cache": noise(key_list[5], (BLOCKS, BT, D), 1.0, 6.0, ((0, 128), (2, 4))),
        "block_table": draw_block_table(jax.random.fold_in(key_list[13], 71), 0),
        "lengths": draw_lengths(jax.random.fold_in(key_list[13], 71), 0),
        "out_weight": noise(key_list[8], (D, D), D ** -0.5, 0.109375, ((0, 4), (1, 128))),
        "norm_gain": jnp.clip(1.0 + 0.15 * jax.random.normal(key_list[9], (D,), jnp.float32), 0.25, 1.75).astype(jnp.bfloat16),
        "gate_weight": noise(key_list[10], (D, FF), D ** -0.5, 0.109375, ((0, 4), (1, 128))),
        "up_weight": noise(key_list[11], (D, FF), D ** -0.5, 0.109375, ((0, 4), (1, 128))),
        "down_weight": noise(key_list[12], (FF, D), FF ** -0.5, 0.0625, ((0, 128), (1, 4))),
    }


def rotate(values, positions):
    half_size = HD // 2
    inverse_freq = 10000.0 ** (-(2.0 * jnp.arange(half_size, dtype=jnp.float32)) / HD)
    angles = positions.astype(jnp.float32)[:, None, None] * inverse_freq[None, None, :]
    cosine = jnp.cos(angles)
    sine_part = jnp.sin(angles)
    first = values[..., :half_size]
    second = values[..., half_size:]
    return jnp.concatenate([first * cosine - second * sine_part, second * cosine + first * sine_part], -1)

def reference(residual_in, query_new, key_new, value_new, key_cache, value_cache, block_table, lengths, out_weight, norm_gain, gate_weight, up_weight, down_weight):
    requests = residual_in.shape[0]
    score_scale = 1.0 / math.sqrt(HD)
    queries = rotate(query_new.astype(jnp.float32).reshape(requests, H, HD), lengths).astype(jnp.bfloat16)
    new_keys = rotate(key_new.astype(jnp.float32).reshape(requests, H, HD), lengths).astype(jnp.bfloat16)
    new_values = value_new.reshape(requests, H, HD)

    def attend(inputs):
        query_row, key_self, value_self, block_row, length = inputs
        picked = jnp.clip(block_row, 0, BLOCKS - 1).astype(jnp.int32)
        key_rows = key_cache[picked].reshape(MAXB * BT, H, HD).astype(jnp.float32)
        value_rows = value_cache[picked].reshape(MAXB * BT, H, HD).astype(jnp.float32)
        scores = jnp.einsum('hd,thd->ht', query_row.astype(jnp.float32), key_rows) * score_scale
        valid_mask = jnp.arange(MAXB * BT, dtype=jnp.int32) < length
        scores = jnp.where(valid_mask[None, :], scores, -1e+30)
        self_score = lax.optimization_barrier(jnp.sum(query_row.astype(jnp.float32) * key_self.astype(jnp.float32), -1)) * score_scale
        maximum = jnp.maximum(lax.optimization_barrier(jnp.max(scores, 1)), self_score)
        weights = jnp.where(valid_mask[None, :], jnp.exp(scores - maximum[:, None]), 0.0)
        self_weight = jnp.exp(self_score - maximum)
        totals = lax.optimization_barrier(jnp.sum(weights, 1)) + self_weight
        weights_low = lax.optimization_barrier(weights.astype(jnp.bfloat16))
        self_low = lax.optimization_barrier(self_weight.astype(jnp.bfloat16))
        numerator = jnp.einsum('ht,thd->hd', weights_low.astype(jnp.float32), value_rows)
        numerator = numerator + self_low.astype(jnp.float32)[:, None] * value_self.astype(jnp.float32)
        return (numerator / totals[:, None]).astype(jnp.bfloat16).reshape(H * HD)
    attended = lax.map(attend, (queries, new_keys, new_values, block_table, lengths))
    head_out = lax.optimization_barrier(jnp.dot(attended, out_weight, preferred_element_type=jnp.float32).astype(jnp.bfloat16))
    residual = residual_in.astype(jnp.float32) + head_out.astype(jnp.float32)
    mean_square = lax.optimization_barrier(jnp.mean(residual * residual, -1, keepdims=True))
    normed = (residual * lax.rsqrt(mean_square + 1e-05) * norm_gain.astype(jnp.float32)).astype(jnp.bfloat16)
    gate = jnp.dot(normed, gate_weight, preferred_element_type=jnp.float32)
    up_part = jnp.dot(normed, up_weight, preferred_element_type=jnp.float32)
    hidden = (jax.nn.silu(gate) * up_part).astype(jnp.bfloat16)
    down_out = jnp.dot(hidden, down_weight, preferred_element_type=jnp.float32)
    return (residual + down_out).astype(jnp.bfloat16)
```

```python
import math

import jax
import jax.numpy as jnp
import numpy as np
from jax import lax
from jax.experimental import pallas as pl
from jax.experimental.pallas import tpu as pltpu
from jax.sharding import PartitionSpec as P

HD = 96
N = 8
X = 4
REQ = 256
DEV = 768
HALF = 384
BLK = 5
BT = 256
FFD = 64
MESH = pl.DeviceIdType.MESH
F32 = jnp.float32
BF16 = jnp.bfloat16


def tables():
    lane = np.arange(1024)
    s, r = lane // 128, lane % 128
    f, core, b = r // 10, (r // 5) % 2, r % 5
    ids = np.stack([((f * 16 + s * 2 + core) * 5 + b), ((s * 16 + f * 2 + core) * 5 + b)])
    ids = np.where(r[None] < 80, ids, -7).astype(np.float32)
    k = np.arange(768)
    s, f, core, i = k // 96, (k // 12) % 8, (k // 6) % 2, k % 6
    feats = []
    for z, y in ((f, s), (s, f)):
        feats.append(384 * (z % 2) + 48 * y + 24 * core + 6 * (z // 2) + i)
    feats = np.stack(feats).astype(np.float32)
    return ids, feats


def rotate(values, positions):
    half_size = values.shape[-1] // 2
    inverse_freq = 10000.0 ** (-(2.0 * jnp.arange(half_size, dtype=F32)) / values.shape[-1])
    angles = positions.astype(F32)[:, None, None] * inverse_freq[None, None, :]
    cosine = jnp.cos(angles)
    sine_part = jnp.sin(angles)
    first = values[..., :half_size]
    second = values[..., half_size:]
    return jnp.concatenate(
        [first * cosine - second * sine_part, second * cosine + first * sine_part], -1
    )


def nt(a, b):
    return lax.dot_general(a, b, (((1,), (1,)), ((), ())), preferred_element_type=F32)


def nn(a, b):
    return jnp.dot(a, b, preferred_element_type=F32)


def iota(shape, dim):
    return lax.broadcasted_iota(jnp.int32, shape, dim)


class Net:
    def __init__(self, send, recv):
        self.p = lax.axis_index("pool")
        self.x = lax.axis_index("mlp")
        self.c = self.p % 2
        self.y = (self.p // 2) % N
        self.z = self.p // (2 * N)
        c = self.c
        self.fi = self.z * (1 - c) + self.y * c
        self.si = self.y * (1 - c) + self.z * c
        self.sib = self.p + 1 - 2 * c
        self.send, self.recv = send, recv
        self.ns = self.nr = 0
        self.sent = []

    def recvs(self, count):
        base = self.nr
        self.nr += count
        return base

    def chip(self, z, y, core):
        return z * (2 * N) + y * 2 + core

    def put(self, src, dst, recv_index, pool, mlp=None):
        copy = pltpu.make_async_remote_copy(
            src_ref=src,
            dst_ref=dst,
            send_sem=self.send.at[self.ns],
            recv_sem=self.recv.at[recv_index],
            device_id=(pool, self.x if mlp is None else mlp),
            device_id_type=MESH,
        )
        self.ns += 1
        copy.start()
        self.sent.append(copy)
        return copy

    def got(self, dst, recv_index):
        pltpu.make_async_remote_copy(
            src_ref=dst,
            dst_ref=dst,
            send_sem=self.send.at[0],
            recv_sem=self.recv.at[recv_index],
            device_id=(self.sib, self.x),
            device_id_type=MESH,
        ).wait_recv()

    def spread(self, src, slots, base, along_first=True, pick=False):
        z, y, c = self.z, self.y, self.c
        own_index = self.fi if along_first else self.si
        for k in range(1, N):
            for d in (0, 1):
                on_z = (d == 0) == along_first
                me = z if on_z else y
                t = (me + k) % N
                pool = self.chip(t, y, d) if on_z else self.chip(z, t, d)
                slot = me * 2 + c
                self.put(
                    src.at[d, t] if pick else src.at[d], slots.at[slot], base + slot, pool
                )
        sib_index = self.si if along_first else self.fi
        slot = sib_index * 2 + c
        self.put(
            src.at[1 - c, sib_index] if pick else src.at[1 - c],
            slots.at[slot],
            base + slot,
            self.sib,
        )
        slots[own_index * 2 + c] = src[c, own_index] if pick else src[c]

    def spread_wait(self, slots, base, own_index):
        own = own_index * 2 + self.c
        for k in range(1, 2 * N):
            slot = (own + k) % (2 * N)
            self.got(slots.at[slot], base + slot)

    def line_send(self, bufs, bases):
        c, si = self.c, self.si
        for k in range(1, N):
            t = (si + k) % N
            pool = self.fi * (16 - 14 * c) + t * (2 + 14 * c) + c
            for view, (b, _) in zip(bufs, bases):
                self.put(view(c, si), view(c, si), b + si, pool)
        for view, (_, b) in zip(bufs, bases):
            self.put(view(c, si), view(c, si), b + si, self.sib)

    def line_forward(self, bufs, bases):
        c, si = self.c, self.si
        for k in range(1, N):
            s = (si + N - k) % N
            for view, (b, b2) in zip(bufs, bases):
                self.got(view(c, s), b + s)
                self.put(view(c, s), view(c, s), b2 + s, self.sib)

    def line_wait(self, bufs, bases):
        c = self.c
        for s in range(N):
            for view, (_, b2) in zip(bufs, bases):
                self.got(view(1 - c, s), b2 + s)


def kernel(
    pay_ref, vr_ref, ids_ref, feat_ref, wo_ref, gain_ref, gate_ref, up_ref, down_ref,
    key_hbm, val_hbm, out_ref,
    kbuf, vbuf, slot1, slot2, line1, line2, g1, gv, gr,
    acc_src, lse_src, acc_slot, lse_slot, acc_line, ga, gl,
    bias, ebuf, attb, wgp, s3_src, s3_slot, h_src, h_slot, h_line, gh,
    gu_buf, sq_buf, dbuf, d_slot, b_src, b_slot,
    send, recv, local,
):
    net = Net(send, recv)
    p, x, c, y, z, fi, si = net.p, net.x, net.c, net.y, net.z, net.fi, net.si
    group = p // 32
    rest = p % 32

    kcopy = pltpu.make_async_copy(key_hbm, kbuf, local.at[0])
    vcopy = pltpu.make_async_copy(val_hbm, vbuf, local.at[1])
    kcopy.start()
    vcopy.start()

    barrier = pltpu.get_barrier_semaphore()

    def hello(pool, mlp):
        pl.semaphore_signal(barrier, inc=1, device_id=(pool, mlp), device_id_type=MESH)

    for k in range(1, N):
        for e in (0, 1):
            hello(net.chip((z + k) % N, y, e), x)
            hello(net.chip(z, (y + k) % N, e), x)
    hello(net.sib, x)
    for k in range(1, X):
        hello(p, (x + k) % X)
    home = group == x
    for k in range(X):

        @pl.when(jnp.logical_not(jnp.logical_and(home, x == k)))
        def _():
            hello(32 * x + rest, k)

    pl.semaphore_wait(barrier, 36 - jnp.where(home, 1, 0))

    r_pay, r_vr = net.recvs(16), net.recvs(16)
    net.spread(pay_ref, slot1, r_pay)
    net.spread(vr_ref, slot2, r_vr)

    q_view = lambda d, s: g1.at[d, s]
    v_view = lambda d, s: gv.at[d, s]
    r_view = lambda d, s: gr.at[d, s]
    q_base = [(net.recvs(N), net.recvs(N))]
    v_base = [(net.recvs(N), net.recvs(N))]
    r_base = [(net.recvs(N), net.recvs(N))]

    net.spread_wait(slot1, r_pay, fi)
    for j in range(16):
        line1[2 * j : 2 * j + 2, :] = slot1[j]
    g1[c, si] = line1[...].astype(BF16)
    net.line_send([q_view], q_base)
    net.spread_wait(slot2, r_vr, fi)
    for j in range(16):
        line2[2 * j : 2 * j + 2, :] = slot2[j]
    gv[c, si] = line2[:, :HALF].astype(BF16)
    gr[c, si] = line2[:, HALF:].astype(BF16)
    net.line_send([v_view], v_base)

    gain = gain_ref[...].astype(F32)
    wg = jnp.concatenate([gate_ref[...].astype(F32).T, up_ref[...].astype(F32).T], 0)
    wg = (wg * gain).astype(BF16)
    for d in (0, 1):
        feat = feat_ref[d : d + 1, :]
        for g in range(6):
            cols = feat[:, 128 * g : 128 * g + 128]
            place = (iota((DEV, 128), 0).astype(F32) == cols).astype(F32).astype(BF16)
            wgp[d, :, 128 * g : 128 * g + 128] = nn(wg, place).astype(BF16)
    wot = wo_ref[...].astype(F32).T.astype(BF16)
    o_row, n_col = iota((REQ, REQ), 0), iota((REQ, REQ), 1)
    nat_row = ((o_row >> 2) & 7) * 32 + (o_row >> 5) * 4 + (o_row & 3)
    nat_col = ((n_col >> 2) & 7) * 32 + (n_col >> 5) * 4 + (n_col & 3)
    to_order0 = (nat_row == n_col).astype(F32).astype(BF16)
    to_natural = (o_row == nat_col).astype(F32).astype(BF16)

    net.line_forward([q_view], q_base)
    net.line_wait([q_view], q_base)

    metas = []
    queries = []
    own_len = None
    sub8 = iota((8, REQ), 0)
    for d in (0, 1):
        meta = g1[d, :, :, HALF:].reshape(REQ, 128).astype(F32)
        metas.append(meta)
        meta_t = meta.T
        tab = 16.0 * meta_t[0:16] + meta_t[16:32]
        onehot = jnp.zeros((8, REQ), F32)
        lens = []
        for b in range(BLK):
            match = (tab[0:8] == (p * BLK + b).astype(F32)).astype(F32)
            row = jnp.max(match, 0, keepdims=True)
            onehot = jnp.where(sub8 == b, row, onehot)
            left = match * (tab[8:9] - 256.0 * sub8.astype(F32))
            lens.append(jnp.sum(jnp.sum(left, 0, keepdims=True), 1, keepdims=True))
        own_len = lens
        queries.append(nn(onehot.astype(BF16), g1[d, :, :, :HALF].reshape(REQ, HALF)))
    lane = iota((8, DEV), 1)
    sub = iota((8, DEV), 0)
    head_mask = jnp.logical_and(lane >= 96 * sub, lane < 96 * sub + 96)
    query = jnp.concatenate(queries, 1)
    kcopy.wait()
    vcopy.wait()
    acc = jnp.zeros((8, DEV), F32)
    lane128 = iota((8, 128), 1)
    tiles = [jnp.zeros((8, 128), F32), jnp.zeros((8, 128), F32)]
    scale = 1.0 / math.sqrt(HD)
    for b in range(BLK):
        wide = jnp.where(head_mask, query[b : b + 1, :], 0.0).astype(BF16)
        scores = nt(wide, kbuf[b]) * scale
        valid = iota((8, BT), 1).astype(F32) < own_len[b]
        scores = jnp.where(valid, scores, -1e30)
        top = jnp.max(scores, 1, keepdims=True)
        weights = jnp.where(valid, jnp.exp(scores - top), 0.0)
        total = jnp.maximum(jnp.sum(weights, 1, keepdims=True), 1.0)
        numer = nn(weights.astype(BF16), vbuf[b]) / total
        row = jnp.sum(jnp.where(head_mask, numer, 0.0), 0, keepdims=True)
        acc = jnp.where(sub == b, row, acc)
        lse = top + jnp.log(total)
        for d, f in ((0, z), (1, y)):
            tiles[d] = jnp.where(lane128 == 10 * f + 5 * c + b, lse, tiles[d])
    for d in (0, 1):
        acc_src[d] = acc[:, HALF * d : HALF * d + HALF].astype(BF16)
        lse_src[d] = tiles[d]

    r_acc, r_lse = net.recvs(16), net.recvs(16)
    net.spread(acc_src, acc_slot, r_acc)
    net.spread(lse_src, lse_slot, r_lse)
    net.line_forward([v_view], v_base)
    for d in (0, 1):
        for s in range(N):
            ga[d, s, 80:128, :] = jnp.zeros((48, HALF), BF16)
    net.spread_wait(acc_slot, r_acc, fi)
    for j in range(16):
        acc_line[5 * j : 5 * j + 5, :] = acc_slot[j].astype(F32)[0:5]
    ga[c, si, 0:80, :] = acc_line[...].astype(BF16)
    net.spread_wait(lse_slot, r_lse, fi)
    line = lse_slot[0]
    for j in range(1, 16):
        line = line + lse_slot[j]
    gl[c, si] = line
    a_views = [lambda d, s: ga.at[d, s, pl.ds(0, 80)], lambda d, s: gl.at[d, s]]
    a_base = [(net.recvs(N), net.recvs(N)), (net.recvs(N), net.recvs(N))]
    net.line_send(a_views, a_base)
    net.line_send([r_view], r_base)

    for d in (0, 1):
        meta = metas[d]
        cols = [16.0 * meta[:, j : j + 1] + meta[:, 16 + j : 17 + j] for j in range(8)]
        for s in range(N):
            ids = ids_ref[d : d + 1, 128 * s : 128 * s + 128]
            hit = cols[0] == ids
            for j in range(1, 8):
                hit = jnp.logical_or(hit, cols[j] == ids)
            bias[d, :, 128 * s : 128 * s + 128] = jnp.where(hit, 0.0, -1e30)

    net.line_wait([v_view], v_base)
    net.line_forward(a_views, a_base)
    net.line_wait(a_views, a_base)

    for d in (0, 1):
        meta = metas[d]
        selfs, totals = [], []
        for h in range(4):
            own = meta[:, 32 + h : 33 + h] + meta[:, 36 + h : 37 + h] + meta[:, 40 + h : 41 + h]
            row = 4 * d + h
            score = jnp.concatenate([gl[d, s, row : row + 1, :] for s in range(N)], 1)
            logits = score + bias[d]
            top = jnp.maximum(jnp.max(logits, 1, keepdims=True), own)
            weights = jnp.exp(logits - top)
            own_weight = jnp.exp(own - top)
            totals.append(jnp.sum(weights, 1, keepdims=True) + own_weight)
            selfs.append(own_weight.astype(BF16).astype(F32))
            ebuf[h] = weights.astype(BF16)
        lane_r = iota((REQ, 128), 1)
        for g in range(3):
            block = ga[d, :, :, 128 * g : 128 * g + 128].reshape(1024, 128)
            low = lane_r < 96 - 32 * g
            numer = jnp.where(low, nn(ebuf[g], block), nn(ebuf[g + 1], block))
            value = gv[d, :, :, 128 * g : 128 * g + 128].reshape(REQ, 128).astype(F32)
            numer = numer + jnp.where(low, selfs[g], selfs[g + 1]) * value
            attb[d, :, 128 * g : 128 * g + 128] = (
                numer / jnp.where(low, totals[g], totals[g + 1])
            ).astype(BF16)
    att0 = nn(to_natural, attb[0]).astype(BF16)
    head = nt(wot[:, :HALF], att0) + nt(wot[:, HALF:], attb[1])

    r_s3 = net.recvs(X)
    for k in range(X):
        s3_src[k] = head[6 * k : 6 * k + 6]
    copies = []
    for k in range(X):
        is_self = jnp.logical_and(home, x == k)
        copies.append(
            pltpu.make_async_remote_copy(
                src_ref=s3_src.at[k],
                dst_ref=s3_slot.at[x],
                send_sem=send.at[net.ns + k],
                recv_sem=recv.at[r_s3 + x],
                device_id=(32 * k + rest, group),
                device_id_type=MESH,
            )
        )

        @pl.when(jnp.logical_not(is_self))
        def _(k=k):
            copies[k].start()

    @pl.when(home)
    def _():
        s3_slot[x] = s3_src[x]

    s3_sends = copies
    net.ns += X
    net.line_forward([r_view], r_base)
    net.line_wait([r_view], r_base)
    feature = 24 * rest + 6 * group + iota((8, HALF), 0)
    inputs = []
    for d in (0, 1):
        pick = jnp.logical_and(
            iota((8, HALF), 1) + HALF * d == feature, iota((8, HALF), 0) < 6
        )
        inputs.append(nt(pick.astype(F32).astype(BF16), gr[d].reshape(REQ, HALF)))
    piece = nt(inputs[0].astype(BF16), to_natural) + inputs[1]
    for k in range(X):

        @pl.when(jnp.logical_not(jnp.logical_and(home, x == k)))
        def _(k=k):
            net.got(s3_slot.at[k], r_s3 + k)

    total = (s3_slot[0] + s3_slot[1]) + (s3_slot[2] + s3_slot[3])
    piece = piece[0:6] + total.astype(BF16).astype(F32)
    h_src[0] = piece[:, :128]
    h_src[1] = piece[:, 128:]

    r_h = net.recvs(16)
    h_base = [(net.recvs(N), net.recvs(N))]
    h_view = lambda d, s: gh.at[d, s]
    net.spread(h_src, h_slot, r_h)
    net.spread_wait(h_slot, r_h, fi)
    for j in range(16):
        h_line[6 * j : 6 * j + 6, :] = h_slot[j]
    gh[c, si] = h_line[...].astype(BF16)
    net.line_send([h_view], h_base)
    net.line_forward([h_view], h_base)
    net.line_wait([h_view], h_base)

    for d in (0, 1):
        resid = gh[d].reshape(DEV, 128)
        gu_buf[x, :, 128 * d : 128 * d + 128] = nn(wgp[d], resid).astype(BF16)
        wide = resid.astype(F32)
        square = jnp.sum(wide * wide, 0, keepdims=True)
        sq_buf[x, :, 128 * d : 128 * d + 128] = jnp.broadcast_to(square, (8, 128))
    r_gu, r_sq = net.recvs(X), net.recvs(X)
    for k in range(1, X):
        net.put(gu_buf.at[x], gu_buf.at[x], r_gu + x, p, (x + k) % X)
        net.put(sq_buf.at[x], sq_buf.at[x], r_sq + x, p, (x + k) % X)
    own_resid = jnp.zeros((8, DEV), F32)
    for d in (0, 1):
        pick = iota((8, 128), 1) + 128 * d == 2 * p + iota((8, 128), 0)
        pick = jnp.logical_and(pick, iota((8, 128), 0) < 2)
        mine = nt(pick.astype(F32).astype(BF16), gh[d].reshape(DEV, 128)).astype(BF16)
        feat = feat_ref[d : d + 1, :]
        parts = []
        for g in range(6):
            place = iota((128, DEV), 0).astype(F32) + 128.0 * g == feat
            parts.append(nt(mine, place.astype(F32).astype(BF16)))
        own_resid = own_resid + jnp.concatenate(parts, 1)
    for k in range(1, X):
        t = (x + k) % X
        net.got(gu_buf.at[t], r_gu + t)
        net.got(sq_buf.at[t], r_sq + t)
    gu = gu_buf[0].astype(F32)
    square = sq_buf[0]
    for k in range(1, X):
        gu = gu + gu_buf[k].astype(F32)
        square = square + sq_buf[k]
    inv = lax.rsqrt(square[0:1] * (1.0 / (X * DEV)) + 1e-05)
    gate = gu[:FFD] * inv
    up = gu[FFD:] * inv
    hidden = gate / (1.0 + jnp.exp(-gate)) * up
    hidden_t = hidden.T.astype(BF16)

    down = down_ref[...]
    rows = [nn(to_order0, hidden_t).astype(BF16), hidden_t]
    for d in (0, 1):
        part = nn(rows[d], down[:, HALF * d : HALF * d + HALF]).astype(BF16)
        for s in range(N):
            dbuf[d, s] = part[32 * s : 32 * s + 32]
    r_d = net.recvs(16)
    net.spread(dbuf, d_slot, r_d, along_first=False, pick=True)
    net.spread_wait(d_slot, r_d, si)
    part = d_slot[0].astype(F32)
    for j in range(1, 16):
        part = part + d_slot[j].astype(F32)
    for f in range(N):
        for e in (0, 1):
            b_src[f, e] = part[4 * f + 2 * e : 4 * f + 2 * e + 2]
    r_b = net.recvs(16)
    own = c * N + fi
    for k in range(1, N):
        t = (fi + k) % N
        for e in (0, 1):
            pool = net.chip(t * (1 - c) + z * c, y * (1 - c) + t * c, e)
            net.put(b_src.at[t, e], b_slot.at[own], r_b + own, pool)
    net.put(b_src.at[fi, 1 - c], b_slot.at[own], r_b + own, net.sib)
    b_slot[own] = b_src[fi, c]
    for k in range(1, 16):
        slot = (own + k) % 16
        net.got(b_slot.at[slot], r_b + slot)
    for d in (0, 1):
        total = b_slot[N * d]
        for f in range(1, N):
            total = total + b_slot[N * d + f]
        out_ref[:, HALF * d : HALF * d + HALF] = (
            own_resid[0:2, HALF * d : HALF * d + HALF] + total
        ).astype(BF16)

    for copy in net.sent:
        copy.wait_send()
    for k in range(X):

        @pl.when(jnp.logical_not(jnp.logical_and(home, x == k)))
        def _(k=k):
            s3_sends[k].wait_send()


SENDS = 420
RECVS = 360


def scratch():
    v = pltpu.VMEM
    return [
        v((BLK, BT, DEV), BF16), v((BLK, BT, DEV), BF16),
        v((16, 2, 512), F32), v((16, 2, DEV), F32), v((32, 512), F32), v((32, DEV), F32),
        v((2, N, 32, 512), BF16), v((2, N, 32, HALF), BF16), v((2, N, 32, HALF), BF16),
        v((2, 8, HALF), BF16), v((2, 8, 128), F32), v((16, 8, HALF), BF16), v((16, 8, 128), F32),
        v((80, HALF), F32), v((2, N, 128, HALF), BF16), v((2, N, 8, 128), F32),
        v((2, REQ, 1024), F32), v((4, REQ, 1024), BF16), v((2, REQ, HALF), BF16),
        v((2, 128, DEV), BF16),
        v((X, 6, REQ), F32), v((X, 6, REQ), F32),
        v((2, 6, 128), F32), v((16, 6, 128), F32), v((96, 128), F32), v((2, N, 96, 128), BF16),
        v((X, 128, REQ), BF16), v((X, 8, REQ), F32),
        v((2, N, 32, HALF), BF16), v((16, 32, HALF), BF16), v((N, 2, 2, HALF), F32), v((16, 2, HALF), F32),
        pltpu.SemaphoreType.DMA((SENDS,)), pltpu.SemaphoreType.DMA((RECVS,)),
        pltpu.SemaphoreType.DMA((2,)),
    ]


def per_device(
    residual_in, query_new, key_new, value_new, key_cache, value_cache, block_table, lengths,
    out_weight, norm_gain, gate_weight, up_weight, down_weight,
):
    heads = DEV // HD
    queries = rotate(query_new.astype(F32).reshape(2, heads, HD), lengths).astype(BF16)
    new_keys = rotate(key_new.astype(F32).reshape(2, heads, HD), lengths).astype(BF16)
    queries = queries.astype(F32)
    self_score = jnp.sum(queries * new_keys.astype(F32), -1) * (1.0 / math.sqrt(HD))
    whole = jnp.concatenate([block_table, lengths[:, None]], 1)
    pad = jnp.zeros((2, 7), F32)
    high = (whole >> 4).astype(F32)
    low = (whole & 15).astype(F32)
    s1 = lax.reduce_precision(self_score, 8, 7)
    s2 = lax.reduce_precision(self_score - s1, 8, 7)
    s3 = lax.reduce_precision(self_score - s1 - s2, 8, 7)
    rest = jnp.zeros((2, 84), F32)
    flat = queries.reshape(2, DEV)
    pay = jnp.stack(
        [
            jnp.concatenate(
                [flat[:, HALF * d : HALF * d + HALF], high, pad, low, pad]
                + [s[:, 4 * d : 4 * d + 4] for s in (s1, s2, s3)]
                + [rest],
                1,
            )
            for d in (0, 1)
        ]
    )
    vr = jnp.stack(
        [
            jnp.concatenate(
                [a[:, HALF * d : HALF * d + HALF] for a in (value_new, residual_in)], 1
            ).astype(F32)
            for d in (0, 1)
        ]
    )
    ids, feats = tables()
    vm = pl.BlockSpec(memory_space=pltpu.VMEM)
    hbm = pl.BlockSpec(memory_space=pl.ANY)
    return pl.pallas_call(
        kernel,
        out_shape=jax.ShapeDtypeStruct((2, DEV), BF16),
        in_specs=[vm] * 9 + [hbm] * 2,
        out_specs=vm,
        scratch_shapes=scratch(),
        compiler_params=pltpu.CompilerParams(
            collective_id=0, has_side_effects=True, vmem_limit_bytes=48 * 1024 * 1024
        ),
        name="layer",
    )(
        pay, vr, jnp.asarray(ids), jnp.asarray(feats), out_weight, norm_gain.reshape(1, DEV),
        gate_weight, up_weight, down_weight, key_cache, value_cache,
    )


def solution(mesh):
    in_specs = (
        P("pool", "mlp"),
        P("pool", "mlp"),
        P("pool", "mlp"),
        P("pool", "mlp"),
        P("pool", None, "mlp"),
        P("pool", None, "mlp"),
        P("pool", None),
        P("pool"),
        P("mlp", "pool"),
        P("mlp"),
        P("mlp", "pool"),
        P("mlp", "pool"),
        P("pool", "mlp"),
    )
    out_specs = P("pool", "mlp")
    return jax.shard_map(
        per_device, mesh=mesh, in_specs=in_specs, out_specs=out_specs, check_vma=False
    )
```

```python
import math

import jax
import jax.numpy as jnp
import numpy as np
from jax import lax
from jax.experimental import pallas as pl
from jax.experimental.pallas import tpu as pltpu
from jax.sharding import PartitionSpec as P

HD = 96
SCALE = 1.0 / math.sqrt(HD)
N = 8
X = 4
REQ = 256
DEV = 768
HALF = 384
BLK = 5
BT = 256
FFD = 64
MESH = pl.DeviceIdType.MESH
F32 = jnp.float32
BF16 = jnp.bfloat16


def tables():
    lane = np.arange(1024)
    s, r = lane // 128, lane % 128
    f, core, b = r // 10, (r // 5) % 2, r % 5
    ids = np.stack([((f * 16 + s * 2 + core) * 5 + b), ((s * 16 + f * 2 + core) * 5 + b)])
    ids = np.where(r[None] < 80, ids, -7).astype(np.float32)
    k = np.arange(768)
    s, f, core, i = k // 96, (k // 12) % 8, (k // 6) % 2, k % 6
    feats = []
    for z, y in ((f, s), (s, f)):
        feats.append(384 * (z % 2) + 48 * y + 24 * core + 6 * (z // 2) + i)
    out = np.zeros((8, 1024), np.float32)
    out[0:2] = ids
    out[2:4, :768] = np.stack(feats)
    half = np.arange(768) % 96
    power = -(2.0 * (half % 48)).astype(np.float32) / np.float32(96)
    out[4, :768] = np.float32(10000.0) ** power
    out[5, :768] = np.where(half < 48, -1.0, 1.0)
    return out


def nt(a, b):
    return lax.dot_general(a, b, (((1,), (1,)), ((), ())), preferred_element_type=F32)


def nn(a, b):
    return jnp.dot(a, b, preferred_element_type=F32)


def iota(shape, dim):
    return lax.broadcasted_iota(jnp.int32, shape, dim)


class Net:
    def __init__(self, send, recv):
        self.p = lax.axis_index("pool")
        self.x = lax.axis_index("mlp")
        self.c = self.p % 2
        self.y = (self.p // 2) % N
        self.z = self.p // (2 * N)
        c = self.c
        self.fi = self.z * (1 - c) + self.y * c
        self.si = self.y * (1 - c) + self.z * c
        self.sib = self.p + 1 - 2 * c
        self.send, self.recv = send, recv
        self.ns = self.nr = 0
        self.sent = []

    def recvs(self, count=1):
        base = self.nr
        self.nr += count
        return base

    def sends(self, ref=None):
        self.ns += 1
        if ref is not None:
            self.sent.append((ref, self.ns - 1))
        return self.ns - 1

    def chip(self, z, y, core):
        return z * (2 * N) + y * 2 + core

    def copy(self, src, dst, s, r, pool, mlp=None):
        return pltpu.make_async_remote_copy(
            src_ref=src,
            dst_ref=dst,
            send_sem=self.send.at[s],
            recv_sem=self.recv.at[r],
            device_id=(pool, self.x if mlp is None else mlp),
            device_id_type=MESH,
        )

    def put(self, *args):
        self.copy(*args).start()

    def got(self, dst, r):
        self.copy(dst, dst, 0, r, self.sib).wait_recv()

    def finish(self):
        for ref, s in self.sent:
            self.copy(ref, ref, s, 0, self.sib).wait_send()

    def spread(self, src, slots, r, along_first=True, pick=False):
        z, y, c = self.z, self.y, self.c
        own_index = self.fi if along_first else self.si
        s = self.sends(slots.at[pl.ds(0, 15)])
        for k in (4, 3, 5, 2, 6, 1, 7):
            for d in (0, 1):
                on_z = (d == 0) == along_first
                me = z if on_z else y
                t = (me + k) % N
                pool = self.chip(t, y, d) if on_z else self.chip(z, t, d)
                self.put(src.at[d, t] if pick else src.at[d], slots.at[me * 2 + c], s, r, pool)
        sib_index = self.si if along_first else self.fi
        part = src.at[1 - c, sib_index] if pick else src.at[1 - c]
        self.put(part, slots.at[sib_index * 2 + c], s, r, self.sib)
        slots[own_index * 2 + c] = src[c, own_index] if pick else src[c]

    def spread_wait(self, slots, r):
        self.got(slots.at[pl.ds(0, 15)], r)

    def line_open(self, view):
        return view, self.recvs(N), self.recvs(), self.sends(view(self.c, 0, 7)), self.sends(view(self.c, 0, 8))

    def line_send(self, *lines):
        c, si = self.c, self.si
        for k in (4, 3, 5, 2, 6, 1, 7):
            t = (si + k) % N
            pool = self.fi * (16 - 14 * c) + t * (2 + 14 * c) + c
            for view, r, _, s, _ in lines:
                self.put(view(c, si, 1), view(c, si, 1), s, r + si, pool)
        for view, _, r, _, s in lines:
            self.put(view(c, si, 1), view(c, si, 1), s, r, self.sib)

    def line_forward(self, *lines):
        c, si = self.c, self.si
        for k in (1, 7, 2, 6, 3, 5, 4):
            t = (si + k) % N
            for view, r, r2, _, s2 in lines:
                self.got(view(c, t, 1), r + t)
                self.put(view(c, t, 1), view(c, t, 1), s2, r2, self.sib)

    def line_wait(self, *lines):
        for view, _, r2, _, _ in lines:
            self.got(view(1 - self.c, 0, 8), r2)


def kernel(
    q_hbm, k_hbm, v_hbm, res_hbm, tab_hbm, len_hbm, const_hbm, wo_hbm, gain_hbm, gate_hbm, up_hbm,
    down_hbm, key_hbm, val_hbm, out_ref,
    q_ref, k_ref, v_ref, res_ref, tab_ref, len_ref, const_ref, wo_ref, gain_ref, gate_ref, up_ref,
    down_ref, kbuf, vbuf,
    pay, vr, slot1, slot2, line1, line2, g1, gv, gr,
    acc_src, lse_src, acc_slot, lse_slot, acc_line, ga, gl,
    bias, ebuf, attb, wgp, s3_src, s3_slot, h_src, h_slot, h_line, gh,
    gu_buf, sq_buf, dbuf, d_slot, b_src, b_slot,
    send, recv, local,
):
    net = Net(send, recv)
    p, x, c, y, z, fi, si = net.p, net.x, net.c, net.y, net.z, net.fi, net.si
    group = p // 32
    rest = p % 32

    pairs = [
        (len_hbm, len_ref), (q_hbm, q_ref), (k_hbm, k_ref), (tab_hbm, tab_ref),
        (const_hbm, const_ref), (v_hbm, v_ref), (res_hbm, res_ref), (gate_hbm, gate_ref),
        (up_hbm, up_ref), (gain_hbm, gain_ref), (wo_hbm, wo_ref), (down_hbm, down_ref),
        (key_hbm, kbuf), (val_hbm, vbuf),
    ]
    loads = [pltpu.make_async_copy(a, b, local.at[i]) for i, (a, b) in enumerate(pairs)]
    for load in loads:
        load.start()

    barrier = pltpu.get_barrier_semaphore()

    def hello(pool, mlp):
        pl.semaphore_signal(barrier, inc=1, device_id=(pool, mlp), device_id_type=MESH)

    for k in range(1, N):
        for e in (0, 1):
            hello(net.chip((z + k) % N, y, e), x)
            hello(net.chip(z, (y + k) % N, e), x)
    hello(net.sib, x)
    for k in range(1, X):
        hello(p, (x + k) % X)
    home = group == x
    for k in range(X):

        @pl.when(jnp.logical_not(jnp.logical_and(home, x == k)))
        def _():
            hello(32 * x + rest, k)

    for load in loads[:7]:
        load.wait()
    row8 = iota((8, DEV), 0)
    where_len = jnp.where(row8 == 0, len_ref[0], len_ref[1]).astype(F32)
    angle = where_len * const_ref[4:5, :DEV]
    sign = jnp.broadcast_to(const_ref[5:6, :DEV], (8, DEV))
    cosine, sine = jnp.cos(angle), jnp.sin(angle) * sign
    turned = []
    for ref in (q_ref, k_ref):
        value = jnp.concatenate([ref[...].astype(F32), jnp.zeros((6, DEV), F32)], 0)
        other = jnp.where(
            sign < 0.0, pltpu.roll(value, DEV - HD // 2, 1), pltpu.roll(value, HD // 2, 1)
        )
        turned.append((value * cosine + other * sine).astype(BF16).astype(F32))
    product = turned[0] * turned[1]
    col8 = iota((8, DEV), 1)
    lane128 = iota((8, 128), 1)
    row128 = iota((8, 128), 0)
    lists = jnp.zeros((8, 128), F32)
    for i in (0, 1):
        for j in range(9):
            value = len_ref[i] if j == 8 else tab_ref[i, j]
            here = jnp.logical_and(row128 == i, lane128 == j)
            lists = jnp.where(here, (value >> 4).astype(F32), lists)
            here = jnp.logical_and(row128 == i, lane128 == 16 + j)
            lists = jnp.where(here, (value & 15).astype(F32), lists)
    for d in (0, 1):
        meta = lists
        for h in range(4):
            head = 4 * d + h
            inside = jnp.logical_and(col8 >= HD * head, col8 < HD * head + HD)
            score = jnp.sum(jnp.where(inside, product, 0.0), 1, keepdims=True) * SCALE
            for t in range(3):
                part = score.astype(BF16).astype(F32)
                meta = jnp.where(lane128 == 32 + 4 * t + h, part, meta)
                score = score - part
        pay[d, :, :HALF] = turned[0][0:2, HALF * d : HALF * d + HALF].astype(BF16)
        pay[d, :, HALF:] = meta[0:2].astype(BF16)
        vr[d, :, :HALF] = v_ref[:, HALF * d : HALF * d + HALF]
        vr[d, :, HALF:] = res_ref[:, HALF * d : HALF * d + HALF]

    pl.semaphore_wait(barrier, 36 - jnp.where(home, 1, 0))

    r_pay, r_vr = net.recvs(), net.recvs()
    net.spread(pay, slot1, r_pay)
    net.spread(vr, slot2, r_vr)
    q_line = net.line_open(lambda d, s, n: g1.at[d, pl.ds(s, n)])
    v_line = net.line_open(lambda d, s, n: gv.at[d, pl.ds(s, n)])
    r_line = net.line_open(lambda d, s, n: gr.at[d, pl.ds(s, n)])

    for load in loads[7:]:
        load.wait()
    gain = gain_ref[...].astype(F32)
    wg = jnp.concatenate([gate_ref[...].astype(F32), up_ref[...].astype(F32)], 0)
    wg = (wg * gain).astype(BF16)
    for d in (0, 1):
        feat = const_ref[2 + d : 3 + d, :DEV]
        for g in range(6):
            cols = feat[:, 128 * g : 128 * g + 128]
            place = (iota((DEV, 128), 0).astype(F32) == cols).astype(F32).astype(BF16)
            wgp[d, :, 128 * g : 128 * g + 128] = nn(wg, place).astype(BF16)
    wot = wo_ref[...]
    o_row, n_col = iota((REQ, REQ), 0), iota((REQ, REQ), 1)
    nat_row = ((o_row >> 2) & 7) * 32 + (o_row >> 5) * 4 + (o_row & 3)
    nat_col = ((n_col >> 2) & 7) * 32 + (n_col >> 5) * 4 + (n_col & 3)
    to_order0 = (nat_row == n_col).astype(F32).astype(BF16)
    to_natural = (o_row == nat_col).astype(F32).astype(BF16)

    net.spread_wait(slot1, r_pay)
    for j in range(16):
        line1[2 * j : 2 * j + 2, :] = slot1[j].astype(F32)
    g1[c, si] = line1[...].astype(BF16)
    net.line_send(q_line)
    net.spread_wait(slot2, r_vr)
    for j in range(16):
        line2[2 * j : 2 * j + 2, :] = slot2[j].astype(F32)
    gv[c, si] = line2[:, :HALF].astype(BF16)
    gr[c, si] = line2[:, HALF:].astype(BF16)
    net.line_forward(q_line)
    net.line_send(v_line)
    net.line_wait(q_line)

    metas = []
    queries = []
    own_len = None
    sub8 = iota((8, REQ), 0)
    for d in (0, 1):
        meta = g1[d, :, :, HALF:].reshape(REQ, 128).astype(F32)
        metas.append(meta)
        meta_t = meta.T
        tab = 16.0 * meta_t[0:16] + meta_t[16:32]
        onehot = jnp.zeros((8, REQ), F32)
        lens = []
        for b in range(BLK):
            match = (tab[0:8] == (p * BLK + b).astype(F32)).astype(F32)
            row = jnp.max(match, 0, keepdims=True)
            onehot = jnp.where(sub8 == b, row, onehot)
            left = match * (tab[8:9] - 256.0 * sub8.astype(F32))
            lens.append(jnp.sum(jnp.sum(left, 0, keepdims=True), 1, keepdims=True))
        own_len = lens
        queries.append(nn(onehot.astype(BF16), g1[d, :, :, :HALF].reshape(REQ, HALF)))
    lane = iota((8, DEV), 1)
    sub = iota((8, DEV), 0)
    head_mask = jnp.logical_and(lane >= 96 * sub, lane < 96 * sub + 96)
    query = jnp.concatenate(queries, 1)
    acc = jnp.zeros((8, DEV), F32)
    tiles = [jnp.zeros((8, 128), F32), jnp.zeros((8, 128), F32)]
    for b in range(BLK):
        wide = jnp.where(head_mask, query[b : b + 1, :], 0.0).astype(BF16)
        scores = nt(wide, kbuf[b]) * SCALE
        valid = iota((8, BT), 1).astype(F32) < own_len[b]
        scores = jnp.where(valid, scores, -1e30)
        top = jnp.max(scores, 1, keepdims=True)
        weights = jnp.where(valid, jnp.exp(scores - top), 0.0)
        total = jnp.maximum(jnp.sum(weights, 1, keepdims=True), 1.0)
        numer = nn(weights.astype(BF16), vbuf[b]) / total
        row = jnp.sum(jnp.where(head_mask, numer, 0.0), 0, keepdims=True)
        acc = jnp.where(sub == b, row, acc)
        lse = top + jnp.log(total)
        for d, f in ((0, z), (1, y)):
            tiles[d] = jnp.where(lane128 == 10 * f + 5 * c + b, lse, tiles[d])
    for d in (0, 1):
        acc_src[d] = acc[:, HALF * d : HALF * d + HALF].astype(BF16)
        lse_src[d] = tiles[d]

    r_acc, r_lse = net.recvs(), net.recvs()
    net.spread(acc_src, acc_slot, r_acc)
    net.spread(lse_src, lse_slot, r_lse)
    a_lines = (
        net.line_open(lambda d, s, n: ga.at[d, pl.ds(s, n), pl.ds(0, 80)]),
        net.line_open(lambda d, s, n: gl.at[d, pl.ds(s, n)]),
    )
    for d in (0, 1):
        meta = metas[d]
        cols = [16.0 * meta[:, j : j + 1] + meta[:, 16 + j : 17 + j] for j in range(8)]
        for s in range(N):
            ids = const_ref[d : d + 1, 128 * s : 128 * s + 128]
            hit = cols[0] == ids
            for j in range(1, 8):
                hit = jnp.logical_or(hit, cols[j] == ids)
            bias[d, :, 128 * s : 128 * s + 128] = jnp.where(hit, 0.0, -1e30)
            ga[d, s, 80:128, :] = jnp.zeros((48, HALF), BF16)
    net.spread_wait(acc_slot, r_acc)
    for j in range(16):
        acc_line[5 * j : 5 * j + 5, :] = acc_slot[j].astype(F32)[0:5]
    ga[c, si, 0:80, :] = acc_line[...].astype(BF16)
    net.spread_wait(lse_slot, r_lse)
    line = lse_slot[0]
    for j in range(1, 16):
        line = line + lse_slot[j]
    gl[c, si] = line
    net.line_send(*a_lines)
    net.line_forward(v_line)
    net.line_forward(*a_lines)
    net.line_send(r_line)
    net.line_wait(v_line)
    net.line_wait(*a_lines)

    for d in (0, 1):
        meta = metas[d]
        selfs, totals = [], []
        for h in range(4):
            own = meta[:, 32 + h : 33 + h] + meta[:, 36 + h : 37 + h] + meta[:, 40 + h : 41 + h]
            row = 4 * d + h
            score = jnp.concatenate([gl[d, s, row : row + 1, :] for s in range(N)], 1)
            logits = score + bias[d]
            top = jnp.maximum(jnp.max(logits, 1, keepdims=True), own)
            weights = jnp.exp(logits - top)
            own_weight = jnp.exp(own - top)
            totals.append(jnp.sum(weights, 1, keepdims=True) + own_weight)
            selfs.append(own_weight.astype(BF16).astype(F32))
            ebuf[h] = weights.astype(BF16)
        lane_r = iota((REQ, 128), 1)
        for g in range(3):
            block = ga[d, :, :, 128 * g : 128 * g + 128].reshape(1024, 128)
            low = lane_r < 96 - 32 * g
            numer = jnp.where(low, nn(ebuf[g], block), nn(ebuf[g + 1], block))
            value = gv[d, :, :, 128 * g : 128 * g + 128].reshape(REQ, 128).astype(F32)
            numer = numer + jnp.where(low, selfs[g], selfs[g + 1]) * value
            attb[d, :, 128 * g : 128 * g + 128] = (
                numer / jnp.where(low, totals[g], totals[g + 1])
            ).astype(BF16)
    att0 = nn(to_natural, attb[0]).astype(BF16)
    head = nt(wot[:, :HALF], att0) + nt(wot[:, HALF:], attb[1])

    r_s3 = net.recvs(X)
    for k in range(X):
        s3_src[k] = head[6 * k : 6 * k + 6]
    copies = []
    for k in range(X):
        is_self = jnp.logical_and(home, x == k)
        copies.append(
            net.copy(
                s3_src.at[k], s3_slot.at[x], net.sends(), r_s3 + x, 32 * k + rest, group
            )
        )

        @pl.when(jnp.logical_not(is_self))
        def _(k=k):
            copies[k].start()

    @pl.when(home)
    def _():
        s3_slot[x] = s3_src[x]

    net.line_forward(r_line)
    net.line_wait(r_line)
    feature = 24 * rest + 6 * group + iota((8, HALF), 0)
    inputs = []
    for d in (0, 1):
        pick = jnp.logical_and(
            iota((8, HALF), 1) + HALF * d == feature, iota((8, HALF), 0) < 6
        )
        inputs.append(nt(pick.astype(F32).astype(BF16), gr[d].reshape(REQ, HALF)))
    piece = nt(inputs[0].astype(BF16), to_natural) + inputs[1]
    for k in range(X):

        @pl.when(jnp.logical_not(jnp.logical_and(home, x == k)))
        def _(k=k):
            net.got(s3_slot.at[k], r_s3 + k)

    total = (s3_slot[0] + s3_slot[1]) + (s3_slot[2] + s3_slot[3])
    piece = piece[0:6] + total.astype(BF16).astype(F32)
    h_src[0] = piece[:, :128]
    h_src[1] = piece[:, 128:]

    r_h = net.recvs()
    net.spread(h_src, h_slot, r_h)
    h_lines = net.line_open(lambda d, s, n: gh.at[d, pl.ds(s, n)])
    net.spread_wait(h_slot, r_h)
    for j in range(16):
        h_line[6 * j : 6 * j + 6, :] = h_slot[j]
    gh[c, si] = h_line[...].astype(BF16)
    net.line_send(h_lines)
    net.line_forward(h_lines)
    net.line_wait(h_lines)

    for d in (0, 1):
        resid = gh[d].reshape(DEV, 128)
        gu_buf[x, :, 128 * d : 128 * d + 128] = nn(wgp[d], resid).astype(BF16)
        wide = resid.astype(F32)
        square = jnp.sum(wide * wide, 0, keepdims=True)
        sq_buf[x, :, 128 * d : 128 * d + 128] = jnp.broadcast_to(square, (8, 128))
    r_gu, r_sq = net.recvs(), net.recvs()
    s_gu, s_sq = net.sends(gu_buf.at[pl.ds(0, 3)]), net.sends(sq_buf.at[pl.ds(0, 3)])
    for k in (2, 1, 3):
        net.put(gu_buf.at[x], gu_buf.at[x], s_gu, r_gu, p, (x + k) % X)
        net.put(sq_buf.at[x], sq_buf.at[x], s_sq, r_sq, p, (x + k) % X)
    own_resid = jnp.zeros((8, DEV), F32)
    for d in (0, 1):
        pick = iota((8, 128), 1) + 128 * d == 2 * p + iota((8, 128), 0)
        pick = jnp.logical_and(pick, iota((8, 128), 0) < 2)
        mine = nt(pick.astype(F32).astype(BF16), gh[d].reshape(DEV, 128)).astype(BF16)
        feat = const_ref[2 + d : 3 + d, :DEV]
        parts = []
        for g in range(6):
            place = iota((128, DEV), 0).astype(F32) + 128.0 * g == feat
            parts.append(nt(mine, place.astype(F32).astype(BF16)))
        own_resid = own_resid + jnp.concatenate(parts, 1)
    net.got(gu_buf.at[pl.ds(0, 3)], r_gu)
    net.got(sq_buf.at[pl.ds(0, 3)], r_sq)
    gu = gu_buf[0].astype(F32)
    square = sq_buf[0]
    for k in range(1, X):
        gu = gu + gu_buf[k].astype(F32)
        square = square + sq_buf[k]
    inv = lax.rsqrt(square[0:1] * (1.0 / (X * DEV)) + 1e-05)
    gate = gu[:FFD] * inv
    up = gu[FFD:] * inv
    hidden = gate / (1.0 + jnp.exp(-gate)) * up
    hidden_t = hidden.T.astype(BF16)

    down = down_ref[...]
    rows = [nn(to_order0, hidden_t).astype(BF16), hidden_t]
    for d in (0, 1):
        part = nn(rows[d], down[:, HALF * d : HALF * d + HALF]).astype(BF16)
        for s in range(N):
            dbuf[d, s] = part[32 * s : 32 * s + 32]
    r_d = net.recvs()
    net.spread(dbuf, d_slot, r_d, along_first=False, pick=True)
    net.spread_wait(d_slot, r_d)
    part = d_slot[0].astype(F32)
    for j in range(1, 16):
        part = part + d_slot[j].astype(F32)
    for f in range(N):
        for e in (0, 1):
            b_src[f, e] = part[4 * f + 2 * e : 4 * f + 2 * e + 2]
    r_b = net.recvs()
    s_b = net.sends(b_slot.at[pl.ds(0, 15)])
    own = c * N + fi
    for k in (4, 3, 5, 2, 6, 1, 7):
        t = (fi + k) % N
        for e in (0, 1):
            pool = net.chip(t * (1 - c) + z * c, y * (1 - c) + t * c, e)
            net.put(b_src.at[t, e], b_slot.at[own], s_b, r_b, pool)
    net.put(b_src.at[fi, 1 - c], b_slot.at[own], s_b, r_b, net.sib)
    b_slot[own] = b_src[fi, c]
    net.got(b_slot.at[pl.ds(0, 15)], r_b)
    for d in (0, 1):
        total = b_slot[N * d]
        for f in range(1, N):
            total = total + b_slot[N * d + f]
        out_ref[:, HALF * d : HALF * d + HALF] = (
            own_resid[0:2, HALF * d : HALF * d + HALF] + total
        ).astype(BF16)

    net.finish()
    for k in range(X):

        @pl.when(jnp.logical_not(jnp.logical_and(home, x == k)))
        def _(k=k):
            copies[k].wait_send()


SENDS = 32
RECVS = 72


def scratch():
    v = pltpu.VMEM
    return [
        v((2, DEV), BF16), v((2, DEV), BF16), v((2, DEV), BF16), v((2, DEV), BF16),
        pltpu.SMEM((2, 8), jnp.int32), pltpu.SMEM((2,), jnp.int32), v((8, 1024), F32),
        v((24, DEV), BF16), v((1, DEV), BF16), v((FFD, DEV), BF16), v((FFD, DEV), BF16),
        v((FFD, DEV), BF16), v((BLK, BT, DEV), BF16), v((BLK, BT, DEV), BF16),
        v((2, 2, 512), BF16), v((2, 2, DEV), BF16),
        v((16, 2, 512), BF16), v((16, 2, DEV), BF16), v((32, 512), F32), v((32, DEV), F32),
        v((2, N, 32, 512), BF16), v((2, N, 32, HALF), BF16), v((2, N, 32, HALF), BF16),
        v((2, 8, HALF), BF16), v((2, 8, 128), F32), v((16, 8, HALF), BF16), v((16, 8, 128), F32),
        v((80, HALF), F32), v((2, N, 128, HALF), BF16), v((2, N, 8, 128), F32),
        v((2, REQ, 1024), F32), v((4, REQ, 1024), BF16), v((2, REQ, HALF), BF16),
        v((2, 128, DEV), BF16),
        v((X, 6, REQ), F32), v((X, 6, REQ), F32),
        v((2, 6, 128), F32), v((16, 6, 128), F32), v((96, 128), F32), v((2, N, 96, 128), BF16),
        v((X, 128, REQ), BF16), v((X, 8, REQ), F32),
        v((2, N, 32, HALF), BF16), v((16, 32, HALF), BF16), v((N, 2, 2, HALF), F32), v((16, 2, HALF), F32),
        pltpu.SemaphoreType.DMA((SENDS,)), pltpu.SemaphoreType.DMA((RECVS,)),
        pltpu.SemaphoreType.DMA((14,)),
    ]


def per_device(
    residual_in, query_new, key_new, value_new, key_cache, value_cache, block_table, lengths,
    out_weight, norm_gain, gate_weight, up_weight, down_weight,
):
    vm = pl.BlockSpec(memory_space=pltpu.VMEM)
    hbm = pl.BlockSpec(memory_space=pl.ANY)
    return pl.pallas_call(
        kernel,
        out_shape=jax.ShapeDtypeStruct((2, DEV), BF16),
        in_specs=[hbm] * 14,
        out_specs=vm,
        scratch_shapes=scratch(),
        compiler_params=pltpu.CompilerParams(
            collective_id=0, has_side_effects=True, vmem_limit_bytes=60 * 1024 * 1024
        ),
        name="layer",
    )(
        query_new, key_new, value_new, residual_in, block_table, lengths, jnp.asarray(tables()),
        out_weight.T, norm_gain.reshape(1, DEV), gate_weight.T, up_weight.T, down_weight,
        key_cache, value_cache,
    )


def solution(mesh):
    in_specs = (
        P("pool", "mlp"),
        P("pool", "mlp"),
        P("pool", "mlp"),
        P("pool", "mlp"),
        P("pool", None, "mlp"),
        P("pool", None, "mlp"),
        P("pool", None),
        P("pool"),
        P("mlp", "pool"),
        P("mlp"),
        P("mlp", "pool"),
        P("mlp", "pool"),
        P("pool", "mlp"),
    )
    out_specs = P("pool", "mlp")
    return jax.shard_map(
        per_device, mesh=mesh, in_specs=in_specs, out_specs=out_specs, check_vma=False
    )
```

```python
import math

import jax
import jax.numpy as jnp
import numpy as np
from jax import lax
from jax.experimental import pallas as pl
from jax.experimental.pallas import tpu as pltpu
from jax.sharding import PartitionSpec as P

HD = 96
SCALE = 1.0 / math.sqrt(HD)
N = 8
X = 4
REQ = 256
DEV = 768
HALF = 384
BLK = 5
BT = 256
FFD = 64
MESH = pl.DeviceIdType.MESH
F32 = jnp.float32
BF16 = jnp.bfloat16


def tables():
    lane = np.arange(1024)
    s, r = lane // 128, lane % 128
    f, core, b = r // 10, (r // 5) % 2, r % 5
    ids = np.stack([((f * 16 + s * 2 + core) * 5 + b), ((s * 16 + f * 2 + core) * 5 + b)])
    ids = np.where(r[None] < 80, ids, -7).astype(np.float32)
    z, y, i = lane // 128, (lane // 16) % 8, lane % 16
    feats = 384 * (z % 2) + 48 * y + 24 * ((z // 2) % 2) + 12 * (z // 4) + i
    feats = np.where(i < 12, feats, -7)
    out = np.zeros((8, 1024), np.float32)
    out[0:2] = ids
    out[2] = feats
    half = np.arange(768) % 96
    power = -(2.0 * (half % 48)).astype(np.float32) / np.float32(96)
    out[4, :768] = np.float32(10000.0) ** power
    out[5, :768] = np.where(half < 48, -1.0, 1.0)
    return out


def hops(k):
    return min(k, N - k)


FAR = sorted(
    [(a, b) for a in range(N) for b in range(N) if a or b], key=lambda k: -hops(k[0]) - hops(k[1])
)


def nt(a, b):
    return lax.dot_general(a, b, (((1,), (1,)), ((), ())), preferred_element_type=F32)


def nn(a, b):
    return jnp.dot(a, b, preferred_element_type=F32)


def iota(shape, dim):
    return lax.broadcasted_iota(jnp.int32, shape, dim)


class Net:
    def __init__(self, send, recv):
        self.p = lax.axis_index("pool")
        self.x = lax.axis_index("mlp")
        self.c = self.p % 2
        self.y = (self.p // 2) % N
        self.z = self.p // (2 * N)
        c = self.c
        self.fi = self.z * (1 - c) + self.y * c
        self.si = self.y * (1 - c) + self.z * c
        self.sib = self.p + 1 - 2 * c
        self.send, self.recv = send, recv
        self.ns = self.nr = 0
        self.sent = []

    def recvs(self, count=1):
        base = self.nr
        self.nr += count
        return base

    def sends(self, ref=None):
        self.ns += 1
        if ref is not None:
            self.sent.append((ref, self.ns - 1))
        return self.ns - 1

    def chip(self, z, y, core):
        return z * (2 * N) + y * 2 + core

    def copy(self, src, dst, s, r, pool, mlp=None):
        return pltpu.make_async_remote_copy(
            src_ref=src,
            dst_ref=dst,
            send_sem=self.send.at[s],
            recv_sem=self.recv.at[r],
            device_id=(pool, self.x if mlp is None else mlp),
            device_id_type=MESH,
        )

    def put(self, *args):
        self.copy(*args).start()

    def got(self, dst, r):
        self.copy(dst, dst, 0, r, self.sib).wait_recv()

    def finish(self):
        for ref, s in self.sent:
            self.copy(ref, ref, s, 0, self.sib).wait_send()

    def spread(self, src, slots, r):
        z, y, c = self.z, self.y, self.c
        s = self.sends(slots.at[pl.ds(0, 15)])
        for k in (4, 3, 5, 2, 6, 1, 7):
            for d in (0, 1):
                me = y if d else z
                t = (me + k) % N
                pool = self.chip(z, t, d) if d else self.chip(t, y, d)
                self.put(src.at[d], slots.at[me * 2 + c], s, r, pool)
        self.put(src.at[1 - c], slots.at[self.si * 2 + c], s, r, self.sib)
        slots[self.fi * 2 + c] = src[c]

    def spread_wait(self, slots, r):
        self.got(slots.at[pl.ds(0, 15)], r)

    def line_open(self, view):
        return view, self.recvs(N), self.recvs(), self.sends(view(self.c, 0, 7)), self.sends(view(self.c, 0, 8))

    def line_send(self, *lines):
        c, si = self.c, self.si
        for k in (4, 3, 5, 2, 6, 1, 7):
            t = (si + k) % N
            pool = self.fi * (16 - 14 * c) + t * (2 + 14 * c) + c
            for view, r, _, s, _ in lines:
                self.put(view(c, si, 1), view(c, si, 1), s, r + si, pool)
        for view, _, r, _, s in lines:
            self.put(view(c, si, 1), view(c, si, 1), s, r, self.sib)

    def line_forward(self, *lines, steps=(1, 7, 2, 6, 3, 5, 4)):
        c, si = self.c, self.si
        for k in steps:
            t = (si + k) % N
            for view, r, r2, _, s2 in lines:
                self.got(view(c, t, 1), r + t)
                self.put(view(c, t, 1), view(c, t, 1), s2, r2, self.sib)

    def line_wait(self, *lines):
        for view, _, r2, _, _ in lines:
            self.got(view(1 - self.c, 0, 8), r2)


def kernel(
    q_hbm, k_hbm, v_hbm, res_hbm, tab_hbm, len_hbm, const_hbm, wo_hbm, gain_hbm, gate_hbm, up_hbm,
    down_hbm, key_hbm, val_hbm, out_ref,
    q_ref, k_ref, v_ref, res_ref, tab_ref, len_ref, const_ref, wo_ref, gain_ref, gate_ref, up_ref,
    down_ref, kbuf, vbuf,
    pay, vr, slot1, slot2, line1, line2, g1, gv, gr,
    acc_src, lse_src, acc_slot, lse_slot, acc_line, ga, gl,
    bias, ebuf, attb, wgp, place, s3_src, s3_slot, g4,
    gu_buf, sq_buf, dbuf, d_slot, b_src, b_slot,
    send, recv, local,
):
    net = Net(send, recv)
    p, x, c, y, z, fi, si = net.p, net.x, net.c, net.y, net.z, net.fi, net.si
    group = p // 32

    pairs = [
        (len_hbm, len_ref), (q_hbm, q_ref), (k_hbm, k_ref), (tab_hbm, tab_ref),
        (const_hbm, const_ref), (v_hbm, v_ref), (res_hbm, res_ref), (gate_hbm, gate_ref),
        (up_hbm, up_ref), (gain_hbm, gain_ref), (wo_hbm, wo_ref), (down_hbm, down_ref),
        (key_hbm, kbuf), (val_hbm, vbuf),
    ]
    loads = [pltpu.make_async_copy(a, b, local.at[i]) for i, (a, b) in enumerate(pairs)]
    for load in loads:
        load.start()

    barrier = pltpu.get_barrier_semaphore()

    def hello(pool, mlp):
        pl.semaphore_signal(barrier, inc=1, device_id=(pool, mlp), device_id_type=MESH)

    for k in range(1, N):
        for e in (0, 1):
            hello(net.chip((z + k) % N, y, e), x)
            hello(net.chip(z, (y + k) % N, e), x)
    hello(net.sib, x)
    for k in range(1, X):
        hello(p, (x + k) % X)
    source = 32 * x + 16 * (z % 2) + 2 * y + group % 2
    home = jnp.logical_and(group == x, group % 2 == c)
    for k in range(X):

        @pl.when(jnp.logical_not(jnp.logical_and(home, x == k)))
        def _():
            hello(source, k)

    for load in loads[:7]:
        load.wait()
    row8 = iota((8, DEV), 0)
    where_len = jnp.where(row8 == 0, len_ref[0], len_ref[1]).astype(F32)
    angle = where_len * const_ref[4:5, :DEV]
    sign = jnp.broadcast_to(const_ref[5:6, :DEV], (8, DEV))
    cosine, sine = jnp.cos(angle), jnp.sin(angle) * sign
    turned = []
    for ref in (q_ref, k_ref):
        value = jnp.concatenate([ref[...].astype(F32), jnp.zeros((6, DEV), F32)], 0)
        other = jnp.where(
            sign < 0.0, pltpu.roll(value, DEV - HD // 2, 1), pltpu.roll(value, HD // 2, 1)
        )
        turned.append((value * cosine + other * sine).astype(BF16).astype(F32))
    product = turned[0] * turned[1]
    col8 = iota((8, DEV), 1)
    lane128 = iota((8, 128), 1)
    row128 = iota((8, 128), 0)
    lists = jnp.zeros((8, 128), F32)
    for i in (0, 1):
        for j in range(9):
            value = len_ref[i] if j == 8 else tab_ref[i, j]
            here = jnp.logical_and(row128 == i, lane128 == j)
            lists = jnp.where(here, (value >> 4).astype(F32), lists)
            here = jnp.logical_and(row128 == i, lane128 == 16 + j)
            lists = jnp.where(here, (value & 15).astype(F32), lists)
    for d in (0, 1):
        meta = lists
        for h in range(4):
            head = 4 * d + h
            inside = jnp.logical_and(col8 >= HD * head, col8 < HD * head + HD)
            score = jnp.sum(jnp.where(inside, product, 0.0), 1, keepdims=True) * SCALE
            for t in range(3):
                part = score.astype(BF16).astype(F32)
                meta = jnp.where(lane128 == 32 + 4 * t + h, part, meta)
                score = score - part
        pay[d, :, :HALF] = turned[0][0:2, HALF * d : HALF * d + HALF].astype(BF16)
        pay[d, :, HALF:] = meta[0:2].astype(BF16)
        vr[d, :, :HALF] = v_ref[:, HALF * d : HALF * d + HALF]
        vr[d, :, HALF:] = res_ref[:, HALF * d : HALF * d + HALF]

    pl.semaphore_wait(barrier, 36 - jnp.where(home, 1, 0))

    r_pay, r_vr = net.recvs(), net.recvs()
    net.spread(pay, slot1, r_pay)
    net.spread(vr, slot2, r_vr)
    q_line = net.line_open(lambda d, s, n: g1.at[d, pl.ds(s, n)])
    v_line = net.line_open(lambda d, s, n: gv.at[d, pl.ds(s, n)])
    r_line = net.line_open(lambda d, s, n: gr.at[d, pl.ds(s, n)])

    o_row, n_col = iota((REQ, REQ), 0), iota((REQ, REQ), 1)
    nat_row = ((o_row >> 1) & 63) * 4 + (o_row >> 7) * 2 + (o_row & 1)
    nat_col = ((n_col >> 2) & 7) * 32 + (n_col >> 5) * 4 + (n_col & 3)
    to_core = (nat_row == n_col).astype(F32).astype(BF16)
    to_natural = (o_row == nat_col).astype(F32).astype(BF16)

    net.spread_wait(slot1, r_pay)
    for j in range(16):
        line1[2 * j : 2 * j + 2, :] = slot1[j].astype(F32)
    g1[c, si] = line1[...].astype(BF16)
    net.line_send(q_line)
    net.spread_wait(slot2, r_vr)
    for j in range(16):
        line2[2 * j : 2 * j + 2, :] = slot2[j].astype(F32)
    gv[c, si] = line2[:, :HALF].astype(BF16)
    gr[c, si] = line2[:, HALF:].astype(BF16)
    net.line_forward(q_line)
    net.line_send(v_line)
    net.line_wait(q_line)

    metas = []
    queries = []
    own_len = None
    sub8 = iota((8, REQ), 0)
    for d in (0, 1):
        meta = g1[d, :, :, HALF:].reshape(REQ, 128).astype(F32)
        metas.append(meta)
        meta_t = meta.T
        tab = 16.0 * meta_t[0:16] + meta_t[16:32]
        onehot = jnp.zeros((8, REQ), F32)
        lens = []
        for b in range(BLK):
            match = (tab[0:8] == (p * BLK + b).astype(F32)).astype(F32)
            row = jnp.max(match, 0, keepdims=True)
            onehot = jnp.where(sub8 == b, row, onehot)
            left = match * (tab[8:9] - 256.0 * sub8.astype(F32))
            lens.append(jnp.sum(jnp.sum(left, 0, keepdims=True), 1, keepdims=True))
        own_len = lens
        queries.append(nn(onehot.astype(BF16), g1[d, :, :, :HALF].reshape(REQ, HALF)))
    lane = iota((8, DEV), 1)
    sub = iota((8, DEV), 0)
    head_mask = jnp.logical_and(lane >= 96 * sub, lane < 96 * sub + 96)
    query = jnp.concatenate(queries, 1)
    for load in loads[7:]:
        load.wait()
    acc = jnp.zeros((8, DEV), F32)
    tiles = [jnp.zeros((8, 128), F32), jnp.zeros((8, 128), F32)]
    for b in range(BLK):
        wide = jnp.where(head_mask, query[b : b + 1, :], 0.0).astype(BF16)
        scores = nt(wide, kbuf[b]) * SCALE
        valid = iota((8, BT), 1).astype(F32) < own_len[b]
        scores = jnp.where(valid, scores, -1e30)
        top = jnp.max(scores, 1, keepdims=True)
        weights = jnp.where(valid, jnp.exp(scores - top), 0.0)
        total = jnp.maximum(jnp.sum(weights, 1, keepdims=True), 1.0)
        numer = nn(weights.astype(BF16), vbuf[b]) / total
        row = jnp.sum(jnp.where(head_mask, numer, 0.0), 0, keepdims=True)
        acc = jnp.where(sub == b, row, acc)
        lse = top + jnp.log(total)
        for d, f in ((0, z), (1, y)):
            tiles[d] = jnp.where(lane128 == 10 * f + 5 * c + b, lse, tiles[d])
    for d in (0, 1):
        acc_src[d] = acc[:, HALF * d : HALF * d + HALF].astype(BF16)
        lse_src[d] = tiles[d]

    r_acc, r_lse = net.recvs(), net.recvs()
    net.spread(acc_src, acc_slot, r_acc)
    net.spread(lse_src, lse_slot, r_lse)
    a_lines = (
        net.line_open(lambda d, s, n: ga.at[d, pl.ds(s, n), pl.ds(0, 80)]),
        net.line_open(lambda d, s, n: gl.at[d, pl.ds(s, n)]),
    )
    for d in (0, 1):
        meta = metas[d]
        cols = [16.0 * meta[:, j : j + 1] + meta[:, 16 + j : 17 + j] for j in range(8)]
        for s in range(N):
            ids = const_ref[d : d + 1, 128 * s : 128 * s + 128]
            hit = cols[0] == ids
            for j in range(1, 8):
                hit = jnp.logical_or(hit, cols[j] == ids)
            bias[d, :, 128 * s : 128 * s + 128] = jnp.where(hit, 0.0, -1e30)
            ga[d, s, 80:128, :] = jnp.zeros((48, HALF), BF16)
    net.spread_wait(acc_slot, r_acc)
    for j in range(16):
        acc_line[5 * j : 5 * j + 5, :] = acc_slot[j].astype(F32)[0:5]
    ga[c, si, 0:80, :] = acc_line[...].astype(BF16)
    net.spread_wait(lse_slot, r_lse)
    line = lse_slot[0]
    for j in range(1, 16):
        line = line + lse_slot[j]
    gl[c, si] = line
    net.line_send(a_lines[1])
    net.line_send(a_lines[0])
    net.line_forward(a_lines[1])
    net.line_forward(v_line)
    net.line_wait(a_lines[1])

    selfs, totals = [], []
    steps = ((1,), (7,), (2,), (6,), (3,), (5,), (4,), ())
    for row in range(8):
        d, h = row // 4, row % 4
        meta = metas[d]
        own = meta[:, 32 + h : 33 + h] + meta[:, 36 + h : 37 + h] + meta[:, 40 + h : 41 + h]
        score = jnp.concatenate([gl[d, s, row : row + 1, :] for s in range(N)], 1)
        logits = score + bias[d]
        top = jnp.maximum(jnp.max(logits, 1, keepdims=True), own)
        weights = jnp.exp(logits - top)
        own_weight = jnp.exp(own - top)
        totals.append(jnp.sum(weights, 1, keepdims=True) + own_weight)
        selfs.append(own_weight.astype(BF16).astype(F32))
        ebuf[row] = weights.astype(BF16)
        net.line_forward(a_lines[0], steps=steps[row])
    net.line_send(r_line)
    net.line_wait(v_line, a_lines[0])

    for d in (0, 1):
        lane_r = iota((REQ, 128), 1)
        for g in range(3):
            block = ga[d, :, :, 128 * g : 128 * g + 128].reshape(1024, 128)
            low = lane_r < 96 - 32 * g
            i = 4 * d + g
            numer = jnp.where(low, nn(ebuf[i], block), nn(ebuf[i + 1], block))
            value = gv[d, :, :, 128 * g : 128 * g + 128].reshape(REQ, 128).astype(F32)
            numer = numer + jnp.where(low, selfs[i], selfs[i + 1]) * value
            attb[d, :, 128 * g : 128 * g + 128] = (
                numer / jnp.where(low, totals[i], totals[i + 1])
            ).astype(BF16)
    att0 = nn(to_natural, attb[0]).astype(BF16)
    head = nt(wo_ref[:, :HALF], att0) + nt(wo_ref[:, HALF:], attb[1])

    r_s3 = net.recvs(X)
    copies = []
    for k in range(X):
        a, b = k // 2, k % 2
        s3_src[k] = head[12 * a : 12 * a + 12, 128 * b : 128 * b + 128]
        pool = net.chip(z % 2 + 2 * c + 4 * a, y, b)
        copies.append(net.copy(s3_src.at[k], s3_slot.at[x], net.sends(), r_s3 + x, pool, group))
    kept = 2 * (z // 4) + c
    for k in range(X):

        @pl.when(jnp.logical_not(jnp.logical_and(home, kept == k)))
        def _(k=k):
            copies[k].start()

    @pl.when(home)
    def _():
        s3_slot[x] = s3_src[kept]

    net.line_forward(r_line)
    net.line_wait(r_line)
    feature = 384 * (z % 2) + 48 * y + 24 * (group % 2) + 12 * (z // 4) + iota((16, HALF), 0)
    inputs = []
    for d in (0, 1):
        pick = jnp.logical_and(
            iota((16, HALF), 1) + HALF * d == feature, iota((16, HALF), 0) < 12
        )
        inputs.append(nt(pick.astype(F32).astype(BF16), gr[d].reshape(REQ, HALF)))
    piece = nt(inputs[0].astype(BF16), to_natural) + inputs[1]
    piece = jnp.where(c == 0, piece[:, :128], piece[:, 128:])
    for k in range(X):

        @pl.when(jnp.logical_not(jnp.logical_and(home, x == k)))
        def _(k=k):
            net.got(s3_slot.at[k], r_s3 + k)

    total = (s3_slot[0] + s3_slot[1]) + (s3_slot[2] + s3_slot[3])
    total = jnp.concatenate([total.astype(BF16).astype(F32), jnp.zeros((4, 128), F32)], 0)
    me = z * N + y
    g4[c, me] = (piece + total).astype(BF16)

    r_h, r_h2 = net.recvs(N), net.recvs()
    s_h, s_h2 = net.sends(g4.at[c, pl.ds(0, 63)]), net.sends(g4.at[c])
    for kz, ky in FAR:
        pool = net.chip((z + kz) % N, (y + ky) % N, c)
        net.put(g4.at[c, me], g4.at[c, me], s_h, r_h + z, pool)
    gain = gain_ref[...].astype(F32)
    wg = jnp.concatenate([gate_ref[...].astype(F32), up_ref[...].astype(F32)], 0)
    wg = (wg * gain).astype(BF16)
    for g in range(8):
        feat = const_ref[2:3, 128 * g : 128 * g + 128]
        spot = (iota((DEV, 128), 0).astype(F32) == feat).astype(F32).astype(BF16)
        place[:, 128 * g : 128 * g + 128] = spot
        wgp[:, 128 * g : 128 * g + 128] = nn(wg, spot).astype(BF16)
    for k in (0, 1, 7, 2, 6, 3, 5, 4):
        t = (z + k) % N
        net.got(g4.at[c, pl.ds(0, 8 if k else 7)], r_h + t)
        line = g4.at[c, pl.ds(t * N, N)]
        net.put(line, line, s_h2, r_h2, net.sib)
    net.got(g4.at[1 - c], r_h2)

    for d in (0, 1):
        resid = g4[d].reshape(1024, 128)
        gu_buf[x, :, 128 * d : 128 * d + 128] = nn(wgp[...], resid).astype(BF16)
        wide = resid.astype(F32)
        square = jnp.sum(wide * wide, 0, keepdims=True)
        sq_buf[x, :, 128 * d : 128 * d + 128] = jnp.broadcast_to(square, (8, 128))
    r_gu, r_sq = net.recvs(), net.recvs()
    s_gu, s_sq = net.sends(gu_buf.at[pl.ds(0, 3)]), net.sends(sq_buf.at[pl.ds(0, 3)])
    for k in (2, 1, 3):
        net.put(gu_buf.at[x], gu_buf.at[x], s_gu, r_gu, p, (x + k) % X)
        net.put(sq_buf.at[x], sq_buf.at[x], s_sq, r_sq, p, (x + k) % X)
    own_resid = jnp.zeros((8, DEV), F32)
    for d in (0, 1):
        pick = iota((8, 128), 1) + 128 * d == 2 * p + iota((8, 128), 0)
        pick = jnp.logical_and(pick, iota((8, 128), 0) < 2)
        mine = nt(pick.astype(F32).astype(BF16), g4[d].reshape(1024, 128)).astype(BF16)
        own_resid = own_resid + nt(mine, place[...])
    net.got(gu_buf.at[pl.ds(0, 3)], r_gu)
    net.got(sq_buf.at[pl.ds(0, 3)], r_sq)
    gu = gu_buf[0].astype(F32)
    square = sq_buf[0]
    for k in range(1, X):
        gu = gu + gu_buf[k].astype(F32)
        square = square + sq_buf[k]
    inv = lax.rsqrt(square[0:1] * (1.0 / (X * DEV)) + 1e-05)
    gate = gu[:FFD] * inv
    up = gu[FFD:] * inv
    hidden = gate / (1.0 + jnp.exp(-gate)) * up
    hidden_t = hidden.T.astype(BF16)

    down = down_ref[...]
    rows = nn(to_core, hidden_t).astype(BF16)
    for e in (0, 1):
        part = nn(rows[128 * e : 128 * e + 128], down).astype(BF16)
        dbuf[e] = part.reshape(N, 16, DEV)
    r_d, r_b = net.recvs(N), net.recvs()
    s_d, s_b = net.sends(dbuf.at[0]), net.sends(b_slot.at[pl.ds(0, 63)])
    order = (4, 3, 5, 2, 6, 1, 7, 0)
    for k in order:
        t = (z + k) % N
        net.put(dbuf.at[1 - c, t], d_slot.at[t], s_d, r_d + t, net.sib)
    for k in order:
        t = (z + k) % N
        net.got(d_slot.at[t], r_d + t)
        part = dbuf[c, t].astype(F32) + d_slot[t].astype(F32)
        for j in range(N):
            b_src[t, j] = part[2 * j : 2 * j + 2].astype(BF16)
        for ky in order:
            if k or ky:
                v = (y + ky) % N
                net.put(b_src.at[t, v], b_slot.at[me], s_b, r_b, net.chip(t, v, c))
    b_slot[me] = b_src[z, y]
    net.got(b_slot.at[pl.ds(0, 63)], r_b)
    sums = [b_slot[j].astype(F32) for j in range(4)]
    for j in range(4, 64):
        sums[j % 4] = sums[j % 4] + b_slot[j].astype(F32)
    total = (sums[0] + sums[1]) + (sums[2] + sums[3])
    out_ref[...] = (own_resid[0:2] + total).astype(BF16)

    net.finish()
    for k in range(X):

        @pl.when(jnp.logical_not(jnp.logical_and(home, kept == k)))
        def _(k=k):
            copies[k].wait_send()


SENDS = 32
RECVS = 80


def scratch():
    v = pltpu.VMEM
    return [
        v((2, DEV), BF16), v((2, DEV), BF16), v((2, DEV), BF16), v((2, DEV), BF16),
        pltpu.SMEM((2, 8), jnp.int32), pltpu.SMEM((2,), jnp.int32), v((8, 1024), F32),
        v((24, DEV), BF16), v((1, DEV), BF16), v((FFD, DEV), BF16), v((FFD, DEV), BF16),
        v((FFD, DEV), BF16), v((BLK, BT, DEV), BF16), v((BLK, BT, DEV), BF16),
        v((2, 2, 512), BF16), v((2, 2, DEV), BF16),
        v((16, 2, 512), BF16), v((16, 2, DEV), BF16), v((32, 512), F32), v((32, DEV), F32),
        v((2, N, 32, 512), BF16), v((2, N, 32, HALF), BF16), v((2, N, 32, HALF), BF16),
        v((2, 8, HALF), BF16), v((2, 8, 128), F32), v((16, 8, HALF), BF16), v((16, 8, 128), F32),
        v((80, HALF), F32), v((2, N, 128, HALF), BF16), v((2, N, 8, 128), F32),
        v((2, REQ, 1024), F32), v((8, REQ, 1024), BF16), v((2, REQ, HALF), BF16),
        v((128, 1024), BF16), v((DEV, 1024), BF16),
        v((X, 12, 128), F32), v((X, 12, 128), F32), v((2, 64, 16, 128), BF16),
        v((X, 128, REQ), BF16), v((X, 8, REQ), F32),
        v((2, N, 16, DEV), BF16), v((N, 16, DEV), BF16), v((N, N, 2, DEV), BF16), v((64, 2, DEV), BF16),
        pltpu.SemaphoreType.DMA((SENDS,)), pltpu.SemaphoreType.DMA((RECVS,)),
        pltpu.SemaphoreType.DMA((14,)),
    ]


def per_device(
    residual_in, query_new, key_new, value_new, key_cache, value_cache, block_table, lengths,
    out_weight, norm_gain, gate_weight, up_weight, down_weight,
):
    vm = pl.BlockSpec(memory_space=pltpu.VMEM)
    hbm = pl.BlockSpec(memory_space=pl.ANY)
    return pl.pallas_call(
        kernel,
        out_shape=jax.ShapeDtypeStruct((2, DEV), BF16),
        in_specs=[hbm] * 14,
        out_specs=vm,
        scratch_shapes=scratch(),
        compiler_params=pltpu.CompilerParams(
            collective_id=0, has_side_effects=True, vmem_limit_bytes=60 * 1024 * 1024
        ),
        name="layer",
    )(
        query_new, key_new, value_new, residual_in, block_table, lengths, jnp.asarray(tables()),
        out_weight.T, norm_gain.reshape(1, DEV), gate_weight.T, up_weight.T, down_weight,
        key_cache, value_cache,
    )


def solution(mesh):
    in_specs = (
        P("pool", "mlp"),
        P("pool", "mlp"),
        P("pool", "mlp"),
        P("pool", "mlp"),
        P("pool", None, "mlp"),
        P("pool", None, "mlp"),
        P("pool", None),
        P("pool"),
        P("mlp", "pool"),
        P("mlp"),
        P("mlp", "pool"),
        P("mlp", "pool"),
        P("pool", "mlp"),
    )
    out_specs = P("pool", "mlp")
    return jax.shard_map(
        per_device, mesh=mesh, in_specs=in_specs, out_specs=out_specs, check_vma=False
    )
```

```python
import math

import jax
import jax.numpy as jnp
import numpy as np
from jax import lax
from jax.experimental import pallas as pl
from jax.experimental.pallas import tpu as pltpu
from jax.sharding import PartitionSpec as P

HD = 96
SCALE = 1.0 / math.sqrt(HD)
N = 8
X = 4
REQ = 256
DEV = 768
HALF = 384
BLK = 5
BT = 256
FFD = 64
MESH = pl.DeviceIdType.MESH
F32 = jnp.float32
BF16 = jnp.bfloat16


def tables():
    lane = np.arange(1024)
    s, r = lane // 128, lane % 128
    f, core, b = r // 10, (r // 5) % 2, r % 5
    ids = np.stack([((f * 16 + s * 2 + core) * 5 + b), ((s * 16 + f * 2 + core) * 5 + b)])
    ids = np.where(r[None] < 80, ids, -7).astype(np.float32)
    z, y, i = lane // 128, (lane // 16) % 8, lane % 16
    feats = 384 * (z % 2) + 48 * y + 24 * ((z // 2) % 2) + 12 * (z // 4) + i
    feats = np.where(i < 12, feats, -7)
    out = np.zeros((8, 1024), np.float32)
    out[0:2] = ids
    out[2] = feats
    half = np.arange(768) % 96
    power = -(2.0 * (half % 48)).astype(np.float32) / np.float32(96)
    out[4, :768] = np.float32(10000.0) ** power
    out[5, :768] = np.where(half < 48, -1.0, 1.0)
    return out


def hops(k):
    return min(k, N - k)


FAR = sorted(
    [(a, b) for a in range(N) for b in range(N) if a or b], key=lambda k: -hops(k[0]) - hops(k[1])
)


def nt(a, b):
    return lax.dot_general(a, b, (((1,), (1,)), ((), ())), preferred_element_type=F32)


def nn(a, b):
    return jnp.dot(a, b, preferred_element_type=F32)


def iota(shape, dim):
    return lax.broadcasted_iota(jnp.int32, shape, dim)


class Net:
    def __init__(self, send, recv):
        self.p = lax.axis_index("pool")
        self.x = lax.axis_index("mlp")
        self.c = self.p % 2
        self.y = (self.p // 2) % N
        self.z = self.p // (2 * N)
        c = self.c
        self.fi = self.z * (1 - c) + self.y * c
        self.si = self.y * (1 - c) + self.z * c
        self.sib = self.p + 1 - 2 * c
        self.send, self.recv = send, recv
        self.ns = self.nr = 0
        self.sent = []

    def recvs(self, count=1):
        base = self.nr
        self.nr += count
        return base

    def sends(self, ref=None):
        self.ns += 1
        if ref is not None:
            self.sent.append((ref, self.ns - 1))
        return self.ns - 1

    def chip(self, z, y, core):
        return z * (2 * N) + y * 2 + core

    def copy(self, src, dst, s, r, pool, mlp=None):
        return pltpu.make_async_remote_copy(
            src_ref=src,
            dst_ref=dst,
            send_sem=self.send.at[s],
            recv_sem=self.recv.at[r],
            device_id=(pool, self.x if mlp is None else mlp),
            device_id_type=MESH,
        )

    def put(self, *args):
        self.copy(*args).start()

    def got(self, dst, r):
        self.copy(dst, dst, 0, r, self.sib).wait_recv()

    def finish(self):
        for ref, s in self.sent:
            self.copy(ref, ref, s, 0, self.sib).wait_send()

    def spread(self, src, slots, r):
        z, y, c = self.z, self.y, self.c
        s = self.sends(slots.at[pl.ds(0, 15)])
        for k in (4, 3, 5, 2, 6, 1, 7):
            for d in (0, 1):
                me = y if d else z
                t = (me + k) % N
                pool = self.chip(z, t, d) if d else self.chip(t, y, d)
                self.put(src.at[d], slots.at[me * 2 + c], s, r, pool)
        self.put(src.at[1 - c], slots.at[self.si * 2 + c], s, r, self.sib)
        slots[self.fi * 2 + c] = src[c]

    def spread_wait(self, slots, r):
        self.got(slots.at[pl.ds(0, 15)], r)

    def line_open(self, view):
        return view, self.recvs(N), self.recvs(), self.sends(view(self.c, 0, 7)), self.sends(view(self.c, 0, 8))

    def line_send(self, *lines):
        c, si = self.c, self.si
        for k in (4, 3, 5, 2, 6, 1, 7):
            t = (si + k) % N
            pool = self.fi * (16 - 14 * c) + t * (2 + 14 * c) + c
            for view, r, _, s, _ in lines:
                self.put(view(c, si, 1), view(c, si, 1), s, r + si, pool)
        for view, _, r, _, s in lines:
            self.put(view(c, si, 1), view(c, si, 1), s, r, self.sib)

    def line_forward(self, *lines, steps=(1, 7, 2, 6, 3, 5, 4)):
        c, si = self.c, self.si
        for k in steps:
            t = (si + k) % N
            for view, r, r2, _, s2 in lines:
                self.got(view(c, t, 1), r + t)
                self.put(view(c, t, 1), view(c, t, 1), s2, r2, self.sib)

    def line_wait(self, *lines):
        for view, _, r2, _, _ in lines:
            self.got(view(1 - self.c, 0, 8), r2)


def kernel(
    q_hbm, k_hbm, v_hbm, res_hbm, tab_hbm, len_hbm, const_hbm, wo_hbm, gain_hbm, gate_hbm, up_hbm,
    down_hbm, key_hbm, val_hbm, out_ref,
    q_ref, k_ref, v_ref, res_ref, tab_ref, len_ref, const_ref, wo_ref, gain_ref, gate_ref, up_ref,
    down_ref, kbuf, vbuf,
    pay, vr, slot1, slot2, line1, line2, g1, gv, gr,
    acc_src, lse_src, acc_slot, lse_slot, acc_line, ga, gl,
    bias, ebuf, attb, wgain, wgp, place, s3_src, s3_slot, g4,
    gu_buf, sq_buf, dbuf, d_slot, b_src, b_slot,
    send, recv, local,
):
    net = Net(send, recv)
    p, x, c, y, z, fi, si = net.p, net.x, net.c, net.y, net.z, net.fi, net.si
    group = p // 32

    pairs = [
        (len_hbm, len_ref), (q_hbm, q_ref), (k_hbm, k_ref), (tab_hbm, tab_ref),
        (const_hbm, const_ref), (v_hbm, v_ref), (res_hbm, res_ref), (gate_hbm, gate_ref),
        (up_hbm, up_ref), (gain_hbm, gain_ref), (wo_hbm, wo_ref), (down_hbm, down_ref),
        (key_hbm, kbuf), (val_hbm, vbuf),
    ]
    loads = [pltpu.make_async_copy(a, b, local.at[i]) for i, (a, b) in enumerate(pairs)]
    for load in loads:
        load.start()

    barrier = pltpu.get_barrier_semaphore()

    def hello(pool, mlp):
        pl.semaphore_signal(barrier, inc=1, device_id=(pool, mlp), device_id_type=MESH)

    for k in range(1, N):
        for e in (0, 1):
            hello(net.chip(z + (1 - c) * ((z + k) % N - z), y + c * ((y + k) % N - y), e), x)
        hello(net.chip(z + c * ((z + k) % N - z), y + (1 - c) * ((y + k) % N - y), c), x)
    hello(net.sib, x)
    for k in range(1, X):
        hello(p, (x + k) % X)
    source = 32 * x + 16 * (z % 2) + 2 * y + group % 2
    home = jnp.logical_and(group == x, group % 2 == c)
    for k in range(X):

        @pl.when(jnp.logical_not(jnp.logical_and(home, x == k)))
        def _():
            hello(source, k)

    for load in loads[:7]:
        load.wait()
    row8 = iota((8, DEV), 0)
    where_len = jnp.where(row8 == 0, len_ref[0], len_ref[1]).astype(F32)
    angle = where_len * const_ref[4:5, :DEV]
    sign = jnp.broadcast_to(const_ref[5:6, :DEV], (8, DEV))
    cosine, sine = jnp.cos(angle), jnp.sin(angle) * sign
    turned = []
    for ref in (q_ref, k_ref):
        value = jnp.concatenate([ref[...].astype(F32), jnp.zeros((6, DEV), F32)], 0)
        other = jnp.where(
            sign < 0.0, pltpu.roll(value, DEV - HD // 2, 1), pltpu.roll(value, HD // 2, 1)
        )
        turned.append((value * cosine + other * sine).astype(BF16).astype(F32))
    product = turned[0] * turned[1]
    col8 = iota((8, DEV), 1)
    lane128 = iota((8, 128), 1)
    row128 = iota((8, 128), 0)
    lists = jnp.zeros((8, 128), F32)
    for i in (0, 1):
        for j in range(9):
            value = len_ref[i] if j == 8 else tab_ref[i, j]
            here = jnp.logical_and(row128 == i, lane128 == j)
            lists = jnp.where(here, (value >> 4).astype(F32), lists)
            here = jnp.logical_and(row128 == i, lane128 == 16 + j)
            lists = jnp.where(here, (value & 15).astype(F32), lists)
    for d in (0, 1):
        meta = lists
        for h in range(4):
            head = 4 * d + h
            inside = jnp.logical_and(col8 >= HD * head, col8 < HD * head + HD)
            score = jnp.sum(jnp.where(inside, product, 0.0), 1, keepdims=True) * SCALE
            for t in range(3):
                part = score.astype(BF16).astype(F32)
                meta = jnp.where(lane128 == 32 + 4 * t + h, part, meta)
                score = score - part
        pay[d, :, :HALF] = turned[0][0:2, HALF * d : HALF * d + HALF].astype(BF16)
        pay[d, :, HALF:] = meta[0:2].astype(BF16)
        vr[d, :, :HALF] = v_ref[:, HALF * d : HALF * d + HALF]
        vr[d, :, HALF:] = res_ref[:, HALF * d : HALF * d + HALF]

    pl.semaphore_wait(barrier, 29 - jnp.where(home, 1, 0))

    r_pay, r_vr = net.recvs(), net.recvs()
    net.spread(pay, slot1, r_pay)
    net.spread(vr, slot2, r_vr)
    q_line = net.line_open(lambda d, s, n: g1.at[d, pl.ds(s, n)])
    v_line = net.line_open(lambda d, s, n: gv.at[d, pl.ds(s, n)])
    r_line = net.line_open(lambda d, s, n: gr.at[d, pl.ds(s, n)])

    o_row, n_col = iota((REQ, REQ), 0), iota((REQ, REQ), 1)
    nat_row = ((o_row >> 1) & 63) * 4 + (o_row >> 7) * 2 + (o_row & 1)
    nat_col = ((n_col >> 2) & 7) * 32 + (n_col >> 5) * 4 + (n_col & 3)
    to_core = (nat_row == n_col).astype(F32).astype(BF16)
    to_natural = (o_row == nat_col).astype(F32).astype(BF16)

    for load in loads[7:10]:
        load.wait()
    gain = gain_ref[...].astype(F32)
    wg = jnp.concatenate([gate_ref[...].astype(F32), up_ref[...].astype(F32)], 0)
    wgain[...] = (wg * gain).astype(BF16)

    def prepare(groups):
        for g in groups:
            feat = const_ref[2:3, 128 * g : 128 * g + 128]
            spot = (iota((DEV, 128), 0).astype(F32) == feat).astype(F32).astype(BF16)
            place[:, 128 * g : 128 * g + 128] = spot
            wgp[:, 128 * g : 128 * g + 128] = nn(wgain[...], spot).astype(BF16)

    prepare(range(4))
    net.spread_wait(slot1, r_pay)
    for j in range(16):
        line1[2 * j : 2 * j + 2, :] = slot1[j].astype(F32)
    g1[c, si] = line1[...].astype(BF16)
    net.line_send(q_line)
    net.spread_wait(slot2, r_vr)
    for j in range(16):
        line2[2 * j : 2 * j + 2, :] = slot2[j].astype(F32)
    gv[c, si] = line2[:, :HALF].astype(BF16)
    gr[c, si] = line2[:, HALF:].astype(BF16)
    net.line_forward(q_line)
    net.line_send(v_line)
    net.line_wait(q_line)

    metas = []
    queries = []
    own_len = None
    sub8 = iota((8, REQ), 0)
    for d in (0, 1):
        meta = g1[d, :, :, HALF:].reshape(REQ, 128).astype(F32)
        metas.append(meta)
        meta_t = meta.T
        tab = 16.0 * meta_t[0:16] + meta_t[16:32]
        onehot = jnp.zeros((8, REQ), F32)
        lens = []
        for b in range(BLK):
            match = (tab[0:8] == (p * BLK + b).astype(F32)).astype(F32)
            row = jnp.max(match, 0, keepdims=True)
            onehot = jnp.where(sub8 == b, row, onehot)
            left = match * (tab[8:9] - 256.0 * sub8.astype(F32))
            lens.append(jnp.sum(jnp.sum(left, 0, keepdims=True), 1, keepdims=True))
        own_len = lens
        queries.append(nn(onehot.astype(BF16), g1[d, :, :, :HALF].reshape(REQ, HALF)))
    lane = iota((8, DEV), 1)
    sub = iota((8, DEV), 0)
    head_mask = jnp.logical_and(lane >= 96 * sub, lane < 96 * sub + 96)
    query = jnp.concatenate(queries, 1)
    for load in loads[10:]:
        load.wait()
    acc = jnp.zeros((8, DEV), F32)
    tiles = [jnp.zeros((8, 128), F32), jnp.zeros((8, 128), F32)]
    for b in range(BLK):
        wide = jnp.where(head_mask, query[b : b + 1, :], 0.0).astype(BF16)
        scores = nt(wide, kbuf[b]) * SCALE
        valid = iota((8, BT), 1).astype(F32) < own_len[b]
        scores = jnp.where(valid, scores, -1e30)
        top = jnp.max(scores, 1, keepdims=True)
        weights = jnp.where(valid, jnp.exp(scores - top), 0.0)
        total = jnp.maximum(jnp.sum(weights, 1, keepdims=True), 1.0)
        numer = nn(weights.astype(BF16), vbuf[b]) / total
        row = jnp.sum(jnp.where(head_mask, numer, 0.0), 0, keepdims=True)
        acc = jnp.where(sub == b, row, acc)
        lse = top + jnp.log(total)
        for d, f in ((0, z), (1, y)):
            tiles[d] = jnp.where(lane128 == 10 * f + 5 * c + b, lse, tiles[d])
    for d in (0, 1):
        acc_src[d] = acc[:, HALF * d : HALF * d + HALF].astype(BF16)
        lse_src[d] = tiles[d]

    r_acc, r_lse = net.recvs(), net.recvs()
    net.spread(acc_src, acc_slot, r_acc)
    net.spread(lse_src, lse_slot, r_lse)
    a_lines = (
        net.line_open(lambda d, s, n: ga.at[d, pl.ds(s, n), pl.ds(0, 80)]),
        net.line_open(lambda d, s, n: gl.at[d, pl.ds(s, n)]),
    )
    for d in (0, 1):
        meta = metas[d]
        cols = [16.0 * meta[:, j : j + 1] + meta[:, 16 + j : 17 + j] for j in range(8)]
        for s in range(N):
            ids = const_ref[d : d + 1, 128 * s : 128 * s + 128]
            hit = cols[0] == ids
            for j in range(1, 8):
                hit = jnp.logical_or(hit, cols[j] == ids)
            bias[d, :, 128 * s : 128 * s + 128] = jnp.where(hit, 0.0, -1e30)
            ga[d, s, 80:128, :] = jnp.zeros((48, HALF), BF16)
    net.spread_wait(acc_slot, r_acc)
    for j in range(16):
        acc_line[5 * j : 5 * j + 5, :] = acc_slot[j].astype(F32)[0:5]
    ga[c, si, 0:80, :] = acc_line[...].astype(BF16)
    net.spread_wait(lse_slot, r_lse)
    line = lse_slot[0]
    for j in range(1, 16):
        line = line + lse_slot[j]
    gl[c, si] = line
    net.line_send(a_lines[1])
    net.line_send(a_lines[0])
    net.line_forward(a_lines[1])
    net.line_forward(v_line)
    net.line_wait(a_lines[1])

    selfs, totals = [], []
    steps = ((1,), (7,), (2,), (6,), (3,), (5,), (4,), ())
    for row in range(8):
        d, h = row // 4, row % 4
        meta = metas[d]
        own = meta[:, 32 + h : 33 + h] + meta[:, 36 + h : 37 + h] + meta[:, 40 + h : 41 + h]
        score = jnp.concatenate([gl[d, s, row : row + 1, :] for s in range(N)], 1)
        logits = score + bias[d]
        top = jnp.maximum(jnp.max(logits, 1, keepdims=True), own)
        weights = jnp.exp(logits - top)
        own_weight = jnp.exp(own - top)
        totals.append(jnp.sum(weights, 1, keepdims=True) + own_weight)
        selfs.append(own_weight.astype(BF16).astype(F32))
        ebuf[row] = weights.astype(BF16)
        net.line_forward(a_lines[0], steps=steps[row])
    net.line_send(r_line)
    net.line_wait(v_line, a_lines[0])

    for d in (0, 1):
        lane_r = iota((REQ, 128), 1)
        for g in range(3):
            block = ga[d, :, :, 128 * g : 128 * g + 128].reshape(1024, 128)
            low = lane_r < 96 - 32 * g
            i = 4 * d + g
            numer = jnp.where(low, nn(ebuf[i], block), nn(ebuf[i + 1], block))
            value = gv[d, :, :, 128 * g : 128 * g + 128].reshape(REQ, 128).astype(F32)
            numer = numer + jnp.where(low, selfs[i], selfs[i + 1]) * value
            attb[d, :, 128 * g : 128 * g + 128] = (
                numer / jnp.where(low, totals[i], totals[i + 1])
            ).astype(BF16)
    att0 = nn(to_natural, attb[0]).astype(BF16)
    head = nt(wo_ref[:, :HALF], att0) + nt(wo_ref[:, HALF:], attb[1])

    r_s3 = net.recvs(X)
    copies = []
    for k in range(X):
        a, b = k // 2, k % 2
        s3_src[k] = head[12 * a : 12 * a + 12, 128 * b : 128 * b + 128]
        pool = net.chip(z % 2 + 2 * c + 4 * a, y, b)
        copies.append(net.copy(s3_src.at[k], s3_slot.at[x], net.sends(), r_s3 + x, pool, group))
    kept = 2 * (z // 4) + c
    for k in range(X):

        @pl.when(jnp.logical_not(jnp.logical_and(home, kept == k)))
        def _(k=k):
            copies[k].start()

    @pl.when(home)
    def _():
        s3_slot[x] = s3_src[kept]

    net.line_forward(r_line)
    prepare(range(4, 8))
    net.line_wait(r_line)
    feature = 384 * (z % 2) + 48 * y + 24 * (group % 2) + 12 * (z // 4) + iota((16, HALF), 0)
    inputs = []
    for d in (0, 1):
        pick = jnp.logical_and(
            iota((16, HALF), 1) + HALF * d == feature, iota((16, HALF), 0) < 12
        )
        inputs.append(nt(pick.astype(F32).astype(BF16), gr[d].reshape(REQ, HALF)))
    piece = nt(inputs[0].astype(BF16), to_natural) + inputs[1]
    piece = jnp.where(c == 0, piece[:, :128], piece[:, 128:])
    for k in range(X):

        @pl.when(jnp.logical_not(jnp.logical_and(home, x == k)))
        def _(k=k):
            net.got(s3_slot.at[k], r_s3 + k)

    total = (s3_slot[0] + s3_slot[1]) + (s3_slot[2] + s3_slot[3])
    total = jnp.concatenate([total.astype(BF16).astype(F32), jnp.zeros((4, 128), F32)], 0)
    me = z * N + y
    g4[c, me] = (piece + total).astype(BF16)

    r_h, r_h2 = net.recvs(N), net.recvs()
    s_h, s_h2 = net.sends(g4.at[c, pl.ds(0, 63)]), net.sends(g4.at[c])
    for kz, ky in FAR:
        pool = net.chip((z + kz) % N, (y + ky) % N, c)
        net.put(g4.at[c, me], g4.at[c, me], s_h, r_h + z, pool)
    for k in (0, 1, 7, 2, 6, 3, 5, 4):
        t = (z + k) % N
        net.got(g4.at[c, pl.ds(0, 8 if k else 7)], r_h + t)
        line = g4.at[c, pl.ds(t * N, N)]
        net.put(line, line, s_h2, r_h2, net.sib)
    net.got(g4.at[1 - c], r_h2)

    r_gu, r_sq = net.recvs(), net.recvs()
    s_gu, s_sq = net.sends(gu_buf.at[pl.ds(0, 3)]), net.sends(sq_buf.at[pl.ds(0, 3)])
    for d in (0, 1):
        resid = g4[d].reshape(1024, 128)
        gu_buf[x, d] = nn(wgp[...], resid).astype(BF16)
        for k in (2, 1, 3):
            net.put(gu_buf.at[x, d], gu_buf.at[x, d], s_gu, r_gu, p, (x + k) % X)
    for d in (0, 1):
        wide = g4[d].reshape(1024, 128).astype(F32)
        square = jnp.sum(wide * wide, 0, keepdims=True)
        sq_buf[x, :, 128 * d : 128 * d + 128] = jnp.broadcast_to(square, (8, 128))
    for k in (2, 1, 3):
        net.put(sq_buf.at[x], sq_buf.at[x], s_sq, r_sq, p, (x + k) % X)
    net.got(gu_buf.at[pl.ds(0, 3)], r_gu)
    net.got(sq_buf.at[pl.ds(0, 3)], r_sq)
    sums = [gu_buf[0, d].astype(F32) for d in (0, 1)]
    square = sq_buf[0]
    for k in range(1, X):
        sums = [sums[d] + gu_buf[k, d].astype(F32) for d in (0, 1)]
        square = square + sq_buf[k]
    gu = jnp.concatenate(sums, 1)
    inv = lax.rsqrt(square[0:1] * (1.0 / (X * DEV)) + 1e-05)
    gate = gu[:FFD] * inv
    up = gu[FFD:] * inv
    hidden = gate / (1.0 + jnp.exp(-gate)) * up
    hidden_t = hidden.T.astype(BF16)

    down = down_ref[...]
    rows = nn(to_core, hidden_t).astype(BF16)
    for e in (0, 1):
        part = nn(rows[128 * e : 128 * e + 128], down).astype(BF16)
        dbuf[e] = part.reshape(N, 16, DEV)
    r_d, r_b = net.recvs(N), net.recvs()
    s_d, s_b = net.sends(dbuf.at[0]), net.sends(b_slot.at[pl.ds(0, 63)])
    order = (4, 3, 5, 2, 6, 1, 7, 0)
    for k in order:
        t = (z + k) % N
        net.put(dbuf.at[1 - c, t], d_slot.at[t], s_d, r_d + t, net.sib)
    for k in order:
        t = (z + k) % N
        net.got(d_slot.at[t], r_d + t)
        part = dbuf[c, t].astype(F32) + d_slot[t].astype(F32)
        for j in range(N):
            b_src[t, j] = part[2 * j : 2 * j + 2].astype(BF16)
        for ky in order:
            if k or ky:
                v = (y + ky) % N
                net.put(b_src.at[t, v], b_slot.at[me], s_b, r_b, net.chip(t, v, c))
    b_slot[me] = b_src[z, y]
    mine = jnp.zeros((8, 1024), F32)
    for d in (0, 1):
        pick = iota((8, 128), 1) + 128 * d == 2 * p + iota((8, 128), 0)
        pick = jnp.logical_and(pick, iota((8, 128), 0) < 2)
        mine = mine + nt(pick.astype(F32).astype(BF16), g4[d].reshape(1024, 128))
    own_resid = nt(mine.astype(BF16), place[...])
    net.got(b_slot.at[pl.ds(0, 63)], r_b)
    sums = [b_slot[j].astype(F32) for j in range(4)]
    for j in range(4, 64):
        sums[j % 4] = sums[j % 4] + b_slot[j].astype(F32)
    total = (sums[0] + sums[1]) + (sums[2] + sums[3])
    out_ref[...] = (own_resid[0:2] + total).astype(BF16)

    net.finish()
    for k in range(X):

        @pl.when(jnp.logical_not(jnp.logical_and(home, kept == k)))
        def _(k=k):
            copies[k].wait_send()


SENDS = 32
RECVS = 80


def scratch():
    v = pltpu.VMEM
    return [
        v((2, DEV), BF16), v((2, DEV), BF16), v((2, DEV), BF16), v((2, DEV), BF16),
        pltpu.SMEM((2, 8), jnp.int32), pltpu.SMEM((2,), jnp.int32), v((8, 1024), F32),
        v((24, DEV), BF16), v((1, DEV), BF16), v((FFD, DEV), BF16), v((FFD, DEV), BF16),
        v((FFD, DEV), BF16), v((BLK, BT, DEV), BF16), v((BLK, BT, DEV), BF16),
        v((2, 2, 512), BF16), v((2, 2, DEV), BF16),
        v((16, 2, 512), BF16), v((16, 2, DEV), BF16), v((32, 512), F32), v((32, DEV), F32),
        v((2, N, 32, 512), BF16), v((2, N, 32, HALF), BF16), v((2, N, 32, HALF), BF16),
        v((2, 8, HALF), BF16), v((2, 8, 128), F32), v((16, 8, HALF), BF16), v((16, 8, 128), F32),
        v((80, HALF), F32), v((2, N, 128, HALF), BF16), v((2, N, 8, 128), F32),
        v((2, REQ, 1024), F32), v((8, REQ, 1024), BF16), v((2, REQ, HALF), BF16),
        v((128, DEV), BF16), v((128, 1024), BF16), v((DEV, 1024), BF16),
        v((X, 12, 128), F32), v((X, 12, 128), F32), v((2, 64, 16, 128), BF16),
        v((X, 2, 128, 128), BF16), v((X, 8, REQ), F32),
        v((2, N, 16, DEV), BF16), v((N, 16, DEV), BF16), v((N, N, 2, DEV), BF16), v((64, 2, DEV), BF16),
        pltpu.SemaphoreType.DMA((SENDS,)), pltpu.SemaphoreType.DMA((RECVS,)),
        pltpu.SemaphoreType.DMA((14,)),
    ]


def per_device(
    residual_in, query_new, key_new, value_new, key_cache, value_cache, block_table, lengths,
    out_weight, norm_gain, gate_weight, up_weight, down_weight,
):
    vm = pl.BlockSpec(memory_space=pltpu.VMEM)
    hbm = pl.BlockSpec(memory_space=pl.ANY)
    return pl.pallas_call(
        kernel,
        out_shape=jax.ShapeDtypeStruct((2, DEV), BF16),
        in_specs=[hbm] * 14,
        out_specs=vm,
        scratch_shapes=scratch(),
        compiler_params=pltpu.CompilerParams(
            collective_id=0, has_side_effects=True, vmem_limit_bytes=60 * 1024 * 1024
        ),
        name="layer",
    )(
        query_new, key_new, value_new, residual_in, block_table, lengths, jnp.asarray(tables()),
        out_weight.T, norm_gain.reshape(1, DEV), gate_weight.T, up_weight.T, down_weight,
        key_cache, value_cache,
    )


def solution(mesh):
    in_specs = (
        P("pool", "mlp"),
        P("pool", "mlp"),
        P("pool", "mlp"),
        P("pool", "mlp"),
        P("pool", None, "mlp"),
        P("pool", None, "mlp"),
        P("pool", None),
        P("pool"),
        P("mlp", "pool"),
        P("mlp"),
        P("mlp", "pool"),
        P("mlp", "pool"),
        P("pool", "mlp"),
    )
    out_specs = P("pool", "mlp")
    return jax.shard_map(
        per_device, mesh=mesh, in_specs=in_specs, out_specs=out_specs, check_vma=False
    )
```
